32 devices in a mesh: ctx: 8 (over z, x), fsdp: 4 (over y, core).
Axes of the slice: x: 2, y: 2, z: 4, core: 2. Of those that a mesh axis runs over, the one named last changes fastest.
Arguments:
- layer_input: bfloat16 [4096, 1024], P(('ctx', 'fsdp')), may hold values from -40 to 40, as said below
- gain_attn: bfloat16 [1024], P('fsdp'), may hold values from 0.25 to 1.75
- w_qkv: bfloat16 [1024, 3072], P('fsdp'), may hold values from -1 to 1
- w_out: bfloat16 [1024, 1024], P('fsdp'), may hold values from -3.5 to 3.5
- gain_mlp: bfloat16 [1024], P('fsdp'), may hold values from 0.25 to 1.75
- w_in: bfloat16 [1024, 5248], P('fsdp'), may hold values from -0.1875 to 0.1875
- w_down: bfloat16 [2624, 1024], P('fsdp'), may hold values from -0.125 to 0.125
- cotangent: bfloat16 [4096, 1024], P(('ctx', 'fsdp')), may hold values from -36 to 36
Outputs:
- layer_output: bfloat16 [4096, 1024], P(('ctx', 'fsdp'))
- d_x: float32 [4096, 1024], P(('ctx', 'fsdp'))
- d_gain_attn: float32 [1024], P('fsdp')
- d_gain_mlp: float32 [1024], P('fsdp')
- d_w_qkv: float32 [1024, 3072], P('fsdp')
- d_w_out: float32 [1024, 1024], P('fsdp')
- d_w_in: float32 [1024, 5248], P('fsdp')
- d_w_down: float32 [2624, 1024], P('fsdp')
The draws below stay inside these ranges and needn't reach their ends.
Inputs may be any that keep to these rules, and one draw needn't show every extreme that they name: `layer_input`: input activations with feature scales and token scales that differ.
All inputs are finite; a program needn't handle non-finite values.
Results may differ from the reference program's by a relative error of at most 0.019.
Values may be sent and summed in bfloat16 or wider, within the bound.
No kernel may reach another device: no remote copies, remote signals or barrier semaphores. Data moves between devices by JAX's collectives and lax.ppermute only.
A program may use at most 448 MiB of HBM per device.

```python
import math
import jax
import jax.numpy as jnp
from jax import lax

D = 1024
H = 16
FF = 2624
HD = 64
SEQ = 4096


def draw_layer_input(key, part):
    keys = jax.random.split(jax.random.fold_in(key, 11), 3)
    base = jnp.clip(jax.random.normal(keys[0], (SEQ, D), jnp.float32), -4.0, 4.0)
    column = jnp.exp(jax.random.uniform(keys[1], (1, D), jnp.float32, 0.0, math.log(10.0)))
    row = jnp.exp(jax.random.uniform(keys[2], (SEQ, 1), jnp.float32, math.log(0.1), 0.0))
    return (base * column * row).astype(jnp.bfloat16)


def draw_cotangent(key, part):
    keys = jax.random.split(jax.random.fold_in(key, 23), 2)
    base = jnp.clip(jax.random.normal(keys[0], (SEQ, D), jnp.float32), -4.0, 4.0)
    rise = 3.0 ** (jnp.arange(SEQ).astype(jnp.float32) / (SEQ - 1))
    row = jnp.exp(jax.random.uniform(keys[1], (SEQ,), jnp.float32, 0.0, math.log(3.0)))
    return (base * (rise * row)[:, None]).astype(jnp.bfloat16)


def draw_w_qkv(key, part):
    keys = jax.random.split(jax.random.fold_in(key, 37), 1)
    weights = jnp.clip(jax.random.normal(keys[0], (D, 3 * D), jnp.float32), -4.0, 4.0) * math.sqrt(1.5 / D)
    return jnp.clip(weights, -1.0, 1.0).astype(jnp.bfloat16)


def block_scale(key, shape, cuts, low, top_value):
    factor_of, own = 1.0, jax.random.fold_in(key, 6)
    for axis_at, parts in cuts:
        draws = jnp.exp(jax.random.uniform(jax.random.fold_in(own, axis_at), (parts,), jnp.float32, low / len(cuts), top_value / len(cuts)))
        factor_of = factor_of * jnp.repeat(draws, shape[axis_at] // parts).reshape([-1 if axis == axis_at else 1 for axis in range(len(shape))])
    return factor_of


def centred(own_key, dims, scale, most, pieces=(), held_as=jnp.bfloat16):
    array = scale * jax.random.normal(own_key, dims, jnp.float32)
    if pieces:
        array = array * block_scale(own_key, dims, pieces, -0.22, 0.18)
    return jnp.clip(array, -most, most).astype(held_as)


def setup_inputs(seed: int = 0) -> dict:
    splits = jax.random.split(jax.random.key(seed), 9)
    return {
        "layer_input": draw_layer_input(jax.random.fold_in(splits[8], 71), 0),
        "gain_attn": jnp.clip(1.0 + 0.15 * jax.random.normal(splits[1], (D,), jnp.float32), 0.25, 1.75).astype(jnp.bfloat16),
        "w_qkv": draw_w_qkv(jax.random.fold_in(splits[8], 71), 0),
        "w_out": centred(splits[3], (D, D), (max(1, 14 * D // SEQ)) ** -0.5, 3.5, ((0, 4),)),
        "gain_mlp": jnp.clip(1.0 + 0.15 * jax.random.normal(splits[4], (D,), jnp.float32), 0.25, 1.75).astype(jnp.bfloat16),
        "w_in": centred(splits[5], (D, 2 * FF), D ** -0.5, 0.1875, ((0, 4),)),
        "w_down": centred(splits[6], (FF, D), FF ** -0.5, 0.125, ((0, 4),)),
        "cotangent": draw_cotangent(jax.random.fold_in(splits[8], 71), 0),
    }


EPS = 1e-05
THETA = 160000.0
SQRT_HALF = 0.7071067811865476
INV_SQRT_TAU = 0.3989422804014327

def layer_norm(values, gain):
    middle = lax.optimization_barrier(jnp.mean(values, axis=-1, keepdims=True))
    centered = values - middle
    spread = lax.optimization_barrier(jnp.mean(centered * centered, axis=-1, keepdims=True))
    inverse = lax.rsqrt(spread + EPS)
    normed = centered * inverse
    return (normed * gain, normed, inverse)

def norm_back(incoming, normed, inverse, gain):
    scaled = incoming * gain
    return inverse * (scaled - lax.optimization_barrier(jnp.mean(scaled, axis=-1, keepdims=True)) - normed * lax.optimization_barrier(jnp.mean(scaled * normed, axis=-1, keepdims=True)))

def rope_tables(positions, width):
    half = width // 2
    freq = THETA ** (-(jnp.arange(half).astype(jnp.float32) * 2.0 / width))
    angle = positions[:, None] * freq[None, :]
    return (jnp.cos(angle), jnp.sin(angle))

def rotate(values, cosine, sine, sign):
    half = values.shape[-1] // 2
    first = values[..., :half]
    second = values[..., half:]
    cos_b = cosine[:, None, :]
    sin_b = sine[:, None, :] * sign
    return jnp.concatenate([first * cos_b - second * sin_b, second * cos_b + first * sin_b], axis=-1)

def gelu_value(inner):
    return 0.5 * inner * (1.0 + lax.erf(inner * SQRT_HALF))

def gelu_slope(inner):
    return 0.5 * (1.0 + lax.erf(inner * SQRT_HALF)) + inner * jnp.exp(-0.5 * inner * inner) * INV_SQRT_TAU

def round_half(values):
    return lax.optimization_barrier(values.astype(jnp.bfloat16)).astype(jnp.float32)

def reference(layer_input, gain_attn, w_qkv, w_out, gain_mlp, w_in, w_down, cotangent):
    seq = layer_input.shape[0]
    xf = layer_input.astype(jnp.float32)
    gain_one = gain_attn.astype(jnp.float32)
    gain_two = gain_mlp.astype(jnp.float32)
    xn1, n1, r1 = layer_norm(xf, gain_one)
    xn1b = xn1.astype(jnp.bfloat16)
    qkv = jnp.dot(xn1b, w_qkv, preferred_element_type=jnp.float32).reshape(seq, 3, H, HD)
    positions = jnp.arange(seq).astype(jnp.float32)
    cosine, sine = rope_tables(positions, HD)
    queries = rotate(qkv[:, 0], cosine, sine, 1.0).astype(jnp.bfloat16)
    keys = rotate(qkv[:, 1], cosine, sine, 1.0).astype(jnp.bfloat16)
    values = qkv[:, 2].astype(jnp.bfloat16)
    block = math.gcd(seq, 512)
    count = seq // block
    keys_f = keys.astype(jnp.float32)
    values_f = values.astype(jnp.float32)

    def forward_block(query_block):
        score = jnp.einsum('qhd,khd->hqk', query_block.astype(jnp.float32), keys_f) * 0.125
        top = lax.optimization_barrier(jnp.max(score, axis=-1, keepdims=True))
        total = lax.optimization_barrier(jnp.sum(jnp.exp(score - top), axis=-1, keepdims=True))
        lse = top + jnp.log(total)
        probs = round_half(jnp.exp(score - lse))
        out = jnp.einsum('hqk,khd->qhd', probs, values_f)
        return (out.astype(jnp.bfloat16), lse[..., 0])
    attended, lse = lax.map(forward_block, queries.reshape(count, block, H, HD))
    attended = attended.reshape(seq, H, HD)
    flat_attended = attended.reshape(seq, D)
    hidden = xf + jnp.dot(flat_attended, w_out, preferred_element_type=jnp.float32)
    xn2, n2, r2 = layer_norm(hidden, gain_two)
    xn2b = xn2.astype(jnp.bfloat16)
    both = jnp.dot(xn2b, w_in, preferred_element_type=jnp.float32)
    act_in = both[:, :FF]
    gate_in = both[:, FF:]
    mixed = (gelu_value(act_in) * gate_in).astype(jnp.bfloat16)
    output = (hidden + jnp.dot(mixed, w_down, preferred_element_type=jnp.float32)).astype(jnp.bfloat16)
    grad_f = cotangent.astype(jnp.float32)
    d_w_down = jnp.dot(mixed.T, cotangent, preferred_element_type=jnp.float32)
    d_mixed = jnp.dot(cotangent, w_down.T, preferred_element_type=jnp.float32)
    d_both = jnp.concatenate([d_mixed * gate_in * gelu_slope(act_in), d_mixed * gelu_value(act_in)], axis=1).astype(jnp.bfloat16)
    d_w_in = jnp.dot(xn2b.T, d_both, preferred_element_type=jnp.float32)
    d_xn2 = jnp.dot(d_both, w_in.T, preferred_element_type=jnp.float32)
    d_gain_mlp = lax.optimization_barrier(jnp.sum(d_xn2 * n2, axis=0))
    d_hidden = grad_f + norm_back(d_xn2, n2, r2, gain_two)
    d_hidden_b = d_hidden.astype(jnp.bfloat16)
    d_w_out = jnp.dot(flat_attended.T, d_hidden_b, preferred_element_type=jnp.float32)
    d_attended = jnp.dot(d_hidden_b, w_out.T, preferred_element_type=jnp.float32).astype(jnp.bfloat16).reshape(seq, H, HD)
    delta = lax.optimization_barrier(jnp.sum(d_attended.astype(jnp.float32) * attended.astype(jnp.float32), axis=-1))

    def backward_block(carry, item):
        d_keys, d_values = carry
        query_block, grad_block, lse_block, delta_block = item
        query_f = query_block.astype(jnp.float32)
        grad_block_f = grad_block.astype(jnp.float32)
        score = jnp.einsum('qhd,khd->hqk', query_f, keys_f) * 0.125
        probs = jnp.exp(score - lse_block[..., None])
        d_probs = jnp.einsum('qhd,khd->hqk', grad_block_f, values_f)
        d_score = round_half(probs * (d_probs - delta_block.T[..., None]))
        d_query = jnp.einsum('hqk,khd->qhd', d_score, keys_f) * 0.125
        d_keys = d_keys + jnp.einsum('hqk,qhd->khd', d_score, query_f) * 0.125
        d_values = d_values + jnp.einsum('hqk,qhd->khd', round_half(probs), grad_block_f)
        return ((d_keys, d_values), d_query)
    zeros = jnp.zeros((seq, H, HD), jnp.float32)
    items = (queries.reshape(count, block, H, HD), d_attended.reshape(count, block, H, HD), lse, delta.reshape(count, block, H))
    (d_keys, d_values), d_queries = lax.scan(backward_block, (zeros, zeros), items)
    d_queries = d_queries.reshape(seq, H, HD)
    d_qkv = jnp.concatenate([rotate(d_queries, cosine, sine, -1.0).reshape(seq, D), rotate(d_keys, cosine, sine, -1.0).reshape(seq, D), d_values.reshape(seq, D)], axis=1).astype(jnp.bfloat16)
    d_w_qkv = jnp.dot(xn1b.T, d_qkv, preferred_element_type=jnp.float32)
    d_xn1 = jnp.dot(d_qkv, w_qkv.T, preferred_element_type=jnp.float32)
    d_gain_attn = lax.optimization_barrier(jnp.sum(d_xn1 * n1, axis=0))
    d_x = d_hidden + norm_back(d_xn1, n1, r1, gain_one)
    return (output, d_x, d_gain_attn, d_gain_mlp, d_w_qkv, d_w_out, d_w_in, d_w_down)
```

```python
import functools
import math

import jax
import jax.numpy as jnp
from jax import lax
from jax.experimental import pallas as pl
from jax.experimental.pallas import tpu as pltpu
from jax.sharding import Mesh, PartitionSpec as P

H = 16
HD = 64
EPS = 1e-05
THETA = 160000.0
SQRT_HALF = 0.7071067811865476
INV_SQRT_TAU = 0.3989422804014327
LOG2E = 1.4426950408889634
SCALE = 0.125
C2 = SCALE * LOG2E
F32 = jnp.float32
BF16 = jnp.bfloat16
SLAB = ("lo", "fsdp")


def nt_dot(a, b):
    return lax.dot_general(a, b, (((1,), (1,)), ((), ())), preferred_element_type=F32)


def tn_dot(a, b):
    return lax.dot_general(a, b, (((0,), (0,)), ((), ())), preferred_element_type=F32)


def nn_dot(a, b):
    return jnp.dot(a, b, preferred_element_type=F32)


def layer_norm(values, gain):
    middle = jnp.mean(values, axis=-1, keepdims=True)
    centered = values - middle
    spread = jnp.mean(centered * centered, axis=-1, keepdims=True)
    inverse = lax.rsqrt(spread + EPS)
    normed = centered * inverse
    return (normed * gain, normed, inverse)


def norm_back(incoming, normed, inverse, gain):
    scaled = incoming * gain
    return inverse * (
        scaled
        - jnp.mean(scaled, axis=-1, keepdims=True)
        - normed * jnp.mean(scaled * normed, axis=-1, keepdims=True)
    )


def half_turn(u):
    lane = lax.broadcasted_iota(jnp.int32, u.shape, 1)
    return jnp.where(lane % HD < HD // 2, -pltpu.roll(u, 96, 1), pltpu.roll(u, 32, 1))


def lanes_of(values, head):
    lane = lax.broadcasted_iota(jnp.int32, values.shape, 1)
    return jnp.where((lane >= HD) == (head == 1), values, jnp.zeros_like(values))


def merge(first, second):
    shape = first.shape if first.shape[1] > 1 else (first.shape[0], 128)
    lane = lax.broadcasted_iota(jnp.int32, shape, 1)
    return jnp.where(lane < HD, first, second)


def qkv_kernel(x_ref, g_ref, w_ref, cos_ref, sin_ref, xn_ref, q_ref, kv_ref):
    xn, _, _ = layer_norm(x_ref[...].astype(F32), g_ref[...])
    xnb = xn.astype(BF16)
    xn_ref[...] = xnb
    out = nn_dot(xnb, w_ref[...])
    cos, sin = cos_ref[...], sin_ref[...]
    q, k = out[:, :128], out[:, 128:256]
    q_ref[...] = (q * cos + half_turn(q) * sin).astype(BF16)
    kv_ref[:, :128] = (k * cos + half_turn(k) * sin).astype(BF16)
    kv_ref[:, 128:] = out[:, 256:].astype(BF16)


def qkv_call(x, gain, w, cos, sin, rows=256):
    total, width = x.shape
    return pl.pallas_call(
        qkv_kernel,
        grid=(total // rows,),
        in_specs=[
            pl.BlockSpec((rows, width), lambda i: (i, 0)),
            pl.BlockSpec((1, width), lambda i: (0, 0)),
            pl.BlockSpec(w.shape, lambda i: (0, 0)),
            pl.BlockSpec((rows, 128), lambda i: (i, 0)),
            pl.BlockSpec((rows, 128), lambda i: (i, 0)),
        ],
        out_specs=[
            pl.BlockSpec((rows, width), lambda i: (i, 0)),
            pl.BlockSpec((rows, 128), lambda i: (i, 0)),
            pl.BlockSpec((rows, 256), lambda i: (i, 0)),
        ],
        out_shape=[
            jax.ShapeDtypeStruct((total, width), BF16),
            jax.ShapeDtypeStruct((total, 128), BF16),
            jax.ShapeDtypeStruct((total, 256), BF16),
        ],
        name="qkv_rope",
    )(x, gain, w, cos, sin)


def fwd_kernel(chunk, q_ref, k_ref, v_ref, o_ref, lse_ref):
    q = q_ref[...]
    rows = q.shape[0]
    qs = [lanes_of(q, h) for h in range(2)]

    def step(j, carry):
        at = pl.multiple_of(j * chunk, chunk)
        k = k_ref[pl.ds(at, chunk), :]
        v = v_ref[pl.ds(at, chunk), :]
        new = []
        for h in range(2):
            top, mass, acc = carry[h]
            s = nt_dot(qs[h], k)
            new_top = jnp.maximum(top, jnp.max(s, axis=1, keepdims=True))
            p = jnp.exp2((s - new_top) * C2)
            keep = jnp.exp2((top - new_top) * C2)
            mass = mass * keep + jnp.sum(p, axis=1, keepdims=True)
            acc = acc * keep + nn_dot(p.astype(BF16), v)
            new.append((new_top, mass, acc))
        return tuple(new)

    start = (
        jnp.full((rows, 1), -jnp.inf, F32),
        jnp.zeros((rows, 1), F32),
        jnp.zeros((rows, 128), F32),
    )
    done = lax.fori_loop(0, k_ref.shape[0] // chunk, step, (start, start))
    o_ref[...] = merge(*[acc / mass for _, mass, acc in done]).astype(BF16)
    lse_ref[...] = merge(*[top * C2 + jnp.log2(mass) for top, mass, _ in done])


def fwd_call(q, kv, rows=256, chunk=1024):
    total, keys = q.shape[0], kv.shape[0]
    return pl.pallas_call(
        functools.partial(fwd_kernel, chunk),
        grid=(total // rows,),
        in_specs=[
            pl.BlockSpec((rows, 128), lambda i: (i, 0)),
            pl.BlockSpec((keys, 128), lambda i: (0, 0)),
            pl.BlockSpec((keys, 128), lambda i: (0, 1)),
        ],
        out_specs=[
            pl.BlockSpec((rows, 128), lambda i: (i, 0)),
            pl.BlockSpec((rows, 128), lambda i: (i, 0)),
        ],
        out_shape=[
            jax.ShapeDtypeStruct((total, 128), BF16),
            jax.ShapeDtypeStruct((total, 128), F32),
        ],
        name="attend",
    )(q, kv, kv)


def column_to_rows(values, parts):
    blocks = values.shape[0] // 128
    flipped = [values[b * 128 : (b + 1) * 128, :].T for b in range(blocks)]
    rows = []
    for h in range(2):
        left = jnp.concatenate([f[h * HD : h * HD + 1, :] for f in flipped], axis=0)
        for _ in range(parts):
            piece = left.astype(BF16)
            rows.append(piece.astype(F32))
            left = left - piece.astype(F32)
    return jnp.concatenate(rows, axis=0).astype(BF16)


def pack_q_kernel(q_ref, lse_ref, out_ref):
    total = q_ref.shape[0]
    out_ref[:total, :] = q_ref[...]
    out_ref[total:, :] = column_to_rows(lse_ref[...], 3)


def pack_g_kernel(g_ref, o_ref, out_ref):
    total = g_ref.shape[0]
    g = g_ref[...]
    out_ref[:total, :] = g
    prod = g.astype(F32) * o_ref[...].astype(F32)
    sums = [jnp.sum(lanes_of(prod, h), axis=1, keepdims=True) for h in range(2)]
    out_ref[total:, :] = column_to_rows(merge(*sums), 2)


def pack_call(kernel, first, second, parts, name):
    total = first.shape[0]
    return pl.pallas_call(
        kernel,
        out_shape=jax.ShapeDtypeStruct((total + total // 128 * 2 * parts, 128), BF16),
        name=name,
    )(first, second)


def dq_kernel(chunk, q_ref, g_ref, o_ref, lse_ref, cos_ref, sin_ref, k_ref, v_ref, dq_ref):
    q, g = q_ref[...], g_ref[...]
    rows = q.shape[0]
    prod = g.astype(F32) * o_ref[...].astype(F32)
    qs = [lanes_of(q, h) for h in range(2)]
    gs = [lanes_of(g, h) for h in range(2)]
    lse = lse_ref[...]
    lses = [lse[:, :1], lse[:, HD : HD + 1]]
    deltas = [jnp.sum(lanes_of(prod, h), axis=1, keepdims=True) for h in range(2)]

    def step(j, carry):
        at = pl.multiple_of(j * chunk, chunk)
        k = k_ref[pl.ds(at, chunk), :]
        v = v_ref[pl.ds(at, chunk), :]
        new = []
        for h in range(2):
            p = jnp.exp2(nt_dot(qs[h], k) * C2 - lses[h])
            ds = (p * (nt_dot(gs[h], v) - deltas[h])).astype(BF16)
            new.append(carry[h] + nn_dot(ds, k))
        return tuple(new)

    zero = jnp.zeros((rows, 128), F32)
    done = lax.fori_loop(0, k_ref.shape[0] // chunk, step, (zero, zero))
    dq = merge(*done) * SCALE
    dq_ref[...] = (dq * cos_ref[...] - half_turn(dq) * sin_ref[...]).astype(BF16)


def dq_call(q, g, o, lse, cos, sin, kv, rows=256, chunk=1024):
    total, keys = q.shape[0], kv.shape[0]
    block = pl.BlockSpec((rows, 128), lambda i: (i, 0))
    return pl.pallas_call(
        functools.partial(dq_kernel, chunk),
        grid=(total // rows,),
        in_specs=[block] * 6
        + [
            pl.BlockSpec((keys, 128), lambda i: (0, 0)),
            pl.BlockSpec((keys, 128), lambda i: (0, 1)),
        ],
        out_specs=block,
        out_shape=jax.ShapeDtypeStruct((total, 128), BF16),
        name="attend_dq",
    )(q, g, o, lse, cos, sin, kv, kv)


def row_of(stats, head, parts, blocks):
    base = head * parts * blocks
    pieces = [stats[base + i * blocks : base + (i + 1) * blocks, :].astype(F32) for i in range(parts)]
    whole = functools.reduce(lambda a, b: a + b, pieces)
    return jnp.concatenate([whole[b : b + 1, :] for b in range(blocks)], axis=1)


def dkv_kernel(k_ref, v_ref, cos_ref, sin_ref, q_ref, g_ref, dk_ref, dv_ref):
    k, v = k_ref[...], v_ref[...]
    rows = k.shape[0]
    ks = [lanes_of(k, h) for h in range(2)]
    vs = [lanes_of(v, h) for h in range(2)]
    blocks = (q_ref.shape[1] - g_ref.shape[1]) // 2
    slab = blocks * 128

    def step(j, carry):
        q = q_ref[j, :slab, :]
        g = g_ref[j, :slab, :]
        lse = q_ref[j, slab:, :].astype(F32)
        delta = g_ref[j, slab:, :].astype(F32)
        new = []
        for h in range(2):
            dk, dv = carry[h]
            p = jnp.exp2(nt_dot(ks[h], q) * C2 - row_of(lse, h, 3, blocks))
            ds = (p * (nt_dot(vs[h], g) - row_of(delta, h, 2, blocks))).astype(BF16)
            dv = dv + nn_dot(p.astype(BF16), g)
            dk = dk + nn_dot(ds, q)
            new.append((dk, dv))
        return tuple(new)

    zero = jnp.zeros((rows, 128), F32)
    done = lax.fori_loop(0, q_ref.shape[0], step, ((zero, zero), (zero, zero)))
    dk = merge(done[0][0], done[1][0]) * SCALE
    dk_ref[...] = (dk * cos_ref[...] - half_turn(dk) * sin_ref[...]).astype(BF16)
    dv_ref[...] = merge(done[0][1], done[1][1]).astype(BF16)


def dkv_call(kv, cos, sin, q_all, g_all, rows=256):
    total = kv.shape[0]
    block = pl.BlockSpec((rows, 128), lambda i: (i, 0))
    return pl.pallas_call(
        dkv_kernel,
        grid=(total // rows,),
        in_specs=[
            block,
            pl.BlockSpec((rows, 128), lambda i: (i, 1)),
            block,
            block,
            pl.BlockSpec(q_all.shape, lambda i: (0, 0, 0)),
            pl.BlockSpec(g_all.shape, lambda i: (0, 0, 0)),
        ],
        out_specs=[block, block],
        out_shape=[jax.ShapeDtypeStruct((total, 128), BF16)] * 2,
        name="attend_dkv",
    )(kv, kv, cos, sin, q_all, g_all)


def gelu_parts(inner):
    phi = 0.5 * (1.0 + lax.erf(inner * SQRT_HALF))
    slope = phi + inner * jnp.exp(-0.5 * inner * inner) * INV_SQRT_TAU
    return inner * phi, slope


def exchange(parts, axes):
    return lax.all_to_all(parts, axes, 0, 0, tiled=True)


def swap_lo(values):
    return lax.ppermute(values, "lo", [(0, 1), (1, 0)])


def pick(values, axis, index):
    return lax.dynamic_index_in_dim(values, index, axis, keepdims=False)


def reduce_lo(pair):
    here = lax.axis_index("lo")
    other = swap_lo(pick(pair, 0, 1 - here).astype(BF16))
    return pick(pair, 0, here) + other.astype(F32)


def both_lo(values):
    here = lax.axis_index("lo")
    other = swap_lo(values)
    first = jnp.where(here == 0, values, other)
    second = jnp.where(here == 0, other, values)
    return jnp.stack([first, second])


def on_device(x, gain_attn, w_qkv, w_out, gain_mlp, w_in, w_down, cotangent):
    lo, nf, hi = lax.axis_size("lo"), lax.axis_size("fsdp"), lax.axis_size("hi")
    rows, width = x.shape
    slab = rows * lo * nf
    here = lax.axis_index("lo")
    ff = w_down.shape[0]

    x_slab = lax.all_gather(x, SLAB, axis=0, tiled=True)
    gains = lax.all_gather(jnp.stack([gain_attn, gain_mlp]), "fsdp", axis=1, tiled=True)
    gain_one, gain_two = gains[:1].astype(F32), gains[1:].astype(F32)
    wq = pick(w_qkv.reshape(-1, 3, nf, lo, 128), 3, here)
    wq = wq.transpose(2, 0, 1, 3).reshape(nf, -1, 384)
    wq = exchange(wq, "fsdp").reshape(width, 384)
    out_full = lax.all_gather(w_out, "fsdp", axis=0, tiled=True)
    wi = w_in.reshape(-1, 2, nf, ff).transpose(2, 1, 0, 3)
    wi = exchange(wi, "fsdp")
    w_a, w_b = wi[:, 0].reshape(width, ff), wi[:, 1].reshape(width, ff)

    first = lax.axis_index("hi") * slab
    half = HD // 2
    freq = THETA ** (-((jnp.arange(128) % half).astype(F32) * 2.0 / HD))
    angle = (first + jnp.arange(slab)).astype(F32)[:, None] * freq[None, :]
    cos, sin = jnp.cos(angle), jnp.sin(angle)

    xn1_slab, q, kv = qkv_call(x_slab, gain_one, wq, cos, sin)
    kv_all = lax.all_gather(kv, "hi", axis=0, tiled=True)
    o, lse = fwd_call(q, kv_all)

    q_pack = pack_call(pack_q_kernel, q, lse, 3, "pack_q")
    q_all = lax.all_gather(q_pack, "hi", axis=0)

    o_own = exchange(o.reshape(lo * nf, rows, 128), SLAB)
    o_own = o_own.reshape(lo, nf, rows, 128).transpose(2, 1, 0, 3).reshape(rows, width)
    xf = x.astype(F32)
    hidden = xf + nn_dot(o_own, out_full)
    xn2, n2, r2 = layer_norm(hidden, gain_two)
    xn2_all = lax.all_gather(xn2.astype(BF16), "fsdp", axis=0, tiled=True)
    ct_all = lax.all_gather(cotangent, "fsdp", axis=0, tiled=True)

    a, b = nn_dot(xn2_all, w_a), nn_dot(xn2_all, w_b)
    act, slope = gelu_parts(a)
    u = (act * b).astype(BF16)
    du = nt_dot(ct_all, w_down)
    da = (du * b * slope).astype(BF16)
    db = (du * act).astype(BF16)

    d_xn2 = (nt_dot(da, w_a) + nt_dot(db, w_b)).astype(BF16).reshape(nf, rows, width)
    d_xn2 = jnp.sum(exchange(d_xn2, "fsdp").astype(F32), axis=0)
    d_hidden = cotangent.astype(F32) + norm_back(d_xn2, n2, r2, gain_two)
    dhb = d_hidden.astype(BF16)
    d_o = nt_dot(dhb, out_full).astype(BF16)
    d_o = d_o.reshape(rows, nf, lo, 128).transpose(2, 1, 0, 3).reshape(lo * nf, rows, 128)
    grads = exchange(d_o, SLAB).reshape(slab, 128)

    g_pack = pack_call(pack_g_kernel, grads, o, 2, "pack_g")
    g_all = lax.all_gather(g_pack, "hi", axis=0)
    dqb = dq_call(q, grads, o, lse, cos, sin, kv_all)
    dkb, dvb = dkv_call(kv, cos, sin, q_all, g_all)

    out_part = nn_dot(u, w_down).astype(BF16).reshape(nf, rows, width)
    out_sum = jnp.sum(exchange(out_part, "fsdp").astype(F32), axis=0)
    output = (hidden + out_sum).astype(BF16)

    p_down = tn_dot(u, ct_all).reshape(ff, lo, width // lo).transpose(1, 0, 2)
    p_down = reduce_lo(p_down).astype(BF16).reshape(ff, hi, -1).transpose(1, 0, 2)
    p_down = lax.psum_scatter(p_down, "hi", scatter_dimension=0, tiled=True)
    p_down = both_lo(lax.all_gather(p_down, "hi", axis=0, tiled=True))
    d_w_down = p_down.transpose(2, 0, 1, 3).reshape(ff, width).astype(F32)

    per = width // nf
    p_in = jnp.stack([tn_dot(xn2_all, da), tn_dot(xn2_all, db)])
    p_in = p_in.reshape(2, nf, lo, hi, -1, ff).transpose(2, 3, 1, 0, 4, 5)
    p_in = reduce_lo(p_in).astype(BF16).reshape(hi, -1, ff)
    p_in = lax.psum_scatter(p_in, "hi", scatter_dimension=0, tiled=True)
    p_in = exchange(p_in.reshape(nf, 2, -1, ff), "fsdp")
    p_in = both_lo(lax.all_gather(p_in, "hi", axis=0))
    d_w_in = p_in.transpose(0, 1, 4, 3, 2, 5).reshape(per, 2 * nf * ff).astype(F32)

    dhb_slab = lax.all_gather(dhb, SLAB, axis=0, tiled=True)
    p_out = tn_dot(o, dhb_slab).astype(BF16)
    p_out = lax.psum_scatter(p_out, "hi", scatter_dimension=0, tiled=True)
    p_out = both_lo(lax.all_gather(p_out, "hi", axis=0, tiled=True))
    d_w_out = p_out.reshape(per, width).astype(F32)

    dqkv = jnp.concatenate([dqb, dkb, dvb], axis=1)
    p_qkv = tn_dot(xn1_slab, dqkv).astype(BF16).reshape(nf, per, 384)
    p_qkv = lax.psum_scatter(p_qkv, "hi", scatter_dimension=1, tiled=True)
    p_qkv = exchange(p_qkv, "fsdp")
    p_qkv = both_lo(lax.all_gather(p_qkv, "hi", axis=0))
    p_qkv = p_qkv.reshape(lo, hi, nf, per // hi, 3, 128).transpose(1, 3, 4, 2, 0, 5)
    d_w_qkv = p_qkv.reshape(per, 3 * width).astype(F32)

    d_xn1 = nt_dot(dqkv, wq).astype(BF16).reshape(lo * nf, rows, width)
    d_xn1 = jnp.sum(exchange(d_xn1, SLAB).astype(F32), axis=0)
    _, n1, r1 = layer_norm(xf, gain_one)
    d_x = d_hidden + norm_back(d_xn1, n1, r1, gain_one)

    d_gain_attn = jnp.sum(w_qkv.astype(F32) * d_w_qkv, axis=1) / gain_attn.astype(F32)
    d_gain_mlp = jnp.sum(w_in.astype(F32) * d_w_in, axis=1) / gain_mlp.astype(F32)
    return (output, d_x, d_gain_attn, d_gain_mlp, d_w_qkv, d_w_out, d_w_in, d_w_down)


def solution(mesh):
    ctx, fsdp = mesh.shape["ctx"], mesh.shape["fsdp"]
    lo = H // 2 // fsdp
    split = Mesh(mesh.devices.reshape(ctx // lo, lo, fsdp), ("hi", "lo", "fsdp"))
    tokens = P(("hi", "lo", "fsdp"), None)
    shards = P("fsdp", None)
    return jax.shard_map(
        on_device,
        mesh=split,
        in_specs=(tokens, P("fsdp"), shards, shards, P("fsdp"), shards, shards, tokens),
        out_specs=(tokens, tokens, P("fsdp"), P("fsdp"), shards, shards, shards, shards),
        check_vma=False,
    )
```

```python
import functools
import math

import jax
import jax.numpy as jnp
from jax import lax
from jax.experimental import pallas as pl
from jax.experimental.pallas import tpu as pltpu
from jax.sharding import Mesh, PartitionSpec as P

H = 16
HD = 64
EPS = 1e-05
THETA = 160000.0
SQRT_HALF = 0.7071067811865476
INV_SQRT_TAU = 0.3989422804014327
LOG2E = 1.4426950408889634
SCALE = 0.125
C2 = SCALE * LOG2E
F32 = jnp.float32
BF16 = jnp.bfloat16
SLAB = ("lo", "fsdp")


def nt_dot(a, b):
    return lax.dot_general(a, b, (((1,), (1,)), ((), ())), preferred_element_type=F32)


def tn_dot(a, b):
    return lax.dot_general(a, b, (((0,), (0,)), ((), ())), preferred_element_type=F32)


def nn_dot(a, b):
    return jnp.dot(a, b, preferred_element_type=F32)


def layer_norm(values, gain):
    middle = jnp.mean(values, axis=-1, keepdims=True)
    centered = values - middle
    spread = jnp.mean(centered * centered, axis=-1, keepdims=True)
    inverse = lax.rsqrt(spread + EPS)
    normed = centered * inverse
    return (normed * gain, normed, inverse)


def norm_back(incoming, normed, inverse, gain):
    scaled = incoming * gain
    return inverse * (
        scaled
        - jnp.mean(scaled, axis=-1, keepdims=True)
        - normed * jnp.mean(scaled * normed, axis=-1, keepdims=True)
    )


def half_turn(u):
    lane = lax.broadcasted_iota(jnp.int32, u.shape, 1)
    return jnp.where(lane % HD < HD // 2, -pltpu.roll(u, 96, 1), pltpu.roll(u, 32, 1))


def lanes_of(values, head):
    lane = lax.broadcasted_iota(jnp.int32, values.shape, 1)
    return jnp.where((lane >= HD) == (head == 1), values, jnp.zeros_like(values))


def merge(first, second):
    shape = first.shape if first.shape[1] > 1 else (first.shape[0], 128)
    lane = lax.broadcasted_iota(jnp.int32, shape, 1)
    return jnp.where(lane < HD, first, second)


def qkv_kernel(x_ref, g_ref, w_ref, cos_ref, sin_ref, xn_ref, q_ref, kv_ref):
    xn, _, _ = layer_norm(x_ref[...].astype(F32), g_ref[...])
    xnb = xn.astype(BF16)
    xn_ref[...] = xnb
    out = nn_dot(xnb, w_ref[...])
    cos, sin = cos_ref[...], sin_ref[...]
    q, k = out[:, :128], out[:, 128:256]
    q_ref[...] = (q * cos + half_turn(q) * sin).astype(BF16)
    kv_ref[:, :128] = (k * cos + half_turn(k) * sin).astype(BF16)
    kv_ref[:, 128:] = out[:, 256:].astype(BF16)


def qkv_call(x, gain, w, cos, sin, rows=256):
    total, width = x.shape
    return pl.pallas_call(
        qkv_kernel,
        grid=(total // rows,),
        in_specs=[
            pl.BlockSpec((rows, width), lambda i: (i, 0)),
            pl.BlockSpec((1, width), lambda i: (0, 0)),
            pl.BlockSpec(w.shape, lambda i: (0, 0)),
            pl.BlockSpec((rows, 128), lambda i: (i, 0)),
            pl.BlockSpec((rows, 128), lambda i: (i, 0)),
        ],
        out_specs=[
            pl.BlockSpec((rows, width), lambda i: (i, 0)),
            pl.BlockSpec((rows, 128), lambda i: (i, 0)),
            pl.BlockSpec((rows, 256), lambda i: (i, 0)),
        ],
        out_shape=[
            jax.ShapeDtypeStruct((total, width), BF16),
            jax.ShapeDtypeStruct((total, 128), BF16),
            jax.ShapeDtypeStruct((total, 256), BF16),
        ],
        name="qkv_rope",
    )(x, gain, w, cos, sin)


def attend_kernel(begin, end, q_ref, k_ref, v_ref, *refs):
    q, k, v = q_ref[...], k_ref[...], v_ref[...]
    rows = q.shape[0]
    if not begin:
        tops, masses, acc = [r[...] for r in refs[:3]]
    new = []
    for h in range(2):
        s = nt_dot(lanes_of(q, h), k)
        top = jnp.max(s, axis=1, keepdims=True)
        if not begin:
            old = tops[:, h * HD : h * HD + 1]
            top = jnp.maximum(old, top)
            keep = jnp.exp2((old - top) * C2)
        p = jnp.exp2((s - top) * C2)
        mass = jnp.sum(p, axis=1, keepdims=True)
        part = nn_dot(p.astype(BF16), v)
        if not begin:
            mass = mass + masses[:, h * HD : h * HD + 1] * keep
            part = part + acc * keep
        new.append((top, mass, part))
    if end:
        refs[-2][...] = merge(*[part / mass for _, mass, part in new]).astype(BF16)
        refs[-1][...] = merge(*[top * C2 + jnp.log2(mass) for top, mass, _ in new])
    else:
        for ref, both in zip(refs[-3:], zip(*new)):
            ref[...] = merge(*both)


def attend_call(q, kv, state, end, rows=256):
    total, keys = q.shape[0], kv.shape[0]
    block = pl.BlockSpec((rows, 128), lambda i: (i, 0))
    shapes = [BF16, F32] if end else [F32] * 3
    work = total * keys * 256 * 4
    return pl.pallas_call(
        functools.partial(attend_kernel, not state, end),
        grid=(total // rows,),
        in_specs=[
            block,
            pl.BlockSpec((keys, 128), lambda i: (0, 0)),
            pl.BlockSpec((keys, 128), lambda i: (0, 1)),
        ]
        + [block] * len(state),
        out_specs=[block] * len(shapes),
        out_shape=[jax.ShapeDtypeStruct((total, 128), t) for t in shapes],
        cost_estimate=pl.CostEstimate(
            flops=work, transcendentals=total * keys * 2, bytes_accessed=total * 4096
        ),
        name="attend",
    )(q, kv, kv, *state)


def column_to_rows(values, parts):
    blocks = values.shape[0] // 128
    flipped = [values[b * 128 : (b + 1) * 128, :].T for b in range(blocks)]
    rows = []
    for h in range(2):
        left = jnp.concatenate([f[h * HD : h * HD + 1, :] for f in flipped], axis=0)
        for _ in range(parts):
            piece = left.astype(BF16)
            rows.append(piece.astype(F32))
            left = left - piece.astype(F32)
    return jnp.concatenate(rows, axis=0).astype(BF16)


def pack_q_kernel(q_ref, lse_ref, out_ref):
    total = q_ref.shape[0]
    out_ref[:total, :] = q_ref[...]
    out_ref[total:, :] = column_to_rows(lse_ref[...], 3)


def pack_g_kernel(g_ref, o_ref, out_ref):
    total = g_ref.shape[0]
    g = g_ref[...]
    out_ref[:total, :] = g
    prod = g.astype(F32) * o_ref[...].astype(F32)
    sums = [jnp.sum(lanes_of(prod, h), axis=1, keepdims=True) for h in range(2)]
    out_ref[total:, :] = column_to_rows(merge(*sums), 2)


def pack_call(kernel, first, second, parts, name):
    total = first.shape[0]
    return pl.pallas_call(
        kernel,
        out_shape=jax.ShapeDtypeStruct((total + total // 128 * 2 * parts, 128), BF16),
        name=name,
    )(first, second)


def dq_kernel(q_ref, g_ref, o_ref, lse_ref, cos_ref, sin_ref, *refs):
    q, g = q_ref[...], g_ref[...]
    prod = g.astype(F32) * o_ref[...].astype(F32)
    lse = lse_ref[...]
    done = []
    for h in range(2):
        qh, gh = lanes_of(q, h), lanes_of(g, h)
        delta = jnp.sum(lanes_of(prod, h), axis=1, keepdims=True)
        total = jnp.zeros(q.shape, F32)
        for kv_ref in refs[:-1]:
            k, v = kv_ref[:, :128], kv_ref[:, 128:]
            p = jnp.exp2(nt_dot(qh, k) * C2 - lse[:, h * HD : h * HD + 1])
            ds = (p * (nt_dot(gh, v) - delta)).astype(BF16)
            total = total + nn_dot(ds, k)
        done.append(total)
    dq = merge(*done) * SCALE
    refs[-1][...] = (dq * cos_ref[...] - half_turn(dq) * sin_ref[...]).astype(BF16)


def dq_call(q, g, o, lse, cos, sin, kvs, part, parts, rows=256):
    total, keys = q.shape[0] // parts, kvs[0].shape[0]
    steps = total // rows
    block = pl.BlockSpec((rows, 128), lambda i: (i + part * steps, 0))
    return pl.pallas_call(
        dq_kernel,
        grid=(steps,),
        in_specs=[block] * 6 + [pl.BlockSpec((keys, 256), lambda i: (0, 0))] * len(kvs),
        out_specs=pl.BlockSpec((rows, 128), lambda i: (i, 0)),
        out_shape=jax.ShapeDtypeStruct((total, 128), BF16),
        cost_estimate=pl.CostEstimate(
            flops=total * keys * len(kvs) * 256 * 6,
            transcendentals=total * keys * len(kvs) * 2,
            bytes_accessed=total * 2048 + keys * len(kvs) * 512,
        ),
        name="attend_dq",
    )(q, g, o, lse, cos, sin, *kvs)


def row_of(stats, head, parts, blocks):
    base = head * parts * blocks
    pieces = [stats[base + i * blocks : base + (i + 1) * blocks, :].astype(F32) for i in range(parts)]
    whole = functools.reduce(lambda a, b: a + b, pieces)
    return jnp.concatenate([whole[b : b + 1, :] for b in range(blocks)], axis=1)


def dkv_kernel(k_ref, v_ref, cos_ref, sin_ref, q_ref, g_ref, dk_ref, dv_ref):
    k, v = k_ref[...], v_ref[...]
    rows = k.shape[0]
    ks = [lanes_of(k, h) for h in range(2)]
    vs = [lanes_of(v, h) for h in range(2)]
    blocks = (q_ref.shape[1] - g_ref.shape[1]) // 2
    slab = blocks * 128

    def step(j, carry):
        q = q_ref[j, :slab, :]
        g = g_ref[j, :slab, :]
        lse = q_ref[j, slab:, :].astype(F32)
        delta = g_ref[j, slab:, :].astype(F32)
        new = []
        for h in range(2):
            dk, dv = carry[h]
            p = jnp.exp2(nt_dot(ks[h], q) * C2 - row_of(lse, h, 3, blocks))
            ds = (p * (nt_dot(vs[h], g) - row_of(delta, h, 2, blocks))).astype(BF16)
            dv = dv + nn_dot(p.astype(BF16), g)
            dk = dk + nn_dot(ds, q)
            new.append((dk, dv))
        return tuple(new)

    zero = jnp.zeros((rows, 128), F32)
    done = lax.fori_loop(0, q_ref.shape[0], step, ((zero, zero), (zero, zero)))
    dk = merge(done[0][0], done[1][0]) * SCALE
    dk_ref[...] = (dk * cos_ref[...] - half_turn(dk) * sin_ref[...]).astype(BF16)
    dv_ref[...] = merge(done[0][1], done[1][1]).astype(BF16)


def dkv_call(kv, cos, sin, q_all, g_all, part, parts, rows=256):
    total = kv.shape[0] // parts
    slab = kv.shape[0] * q_all.shape[0]
    steps = total // rows
    block = pl.BlockSpec((rows, 128), lambda i: (i + part * steps, 0))
    return pl.pallas_call(
        dkv_kernel,
        grid=(steps,),
        in_specs=[
            block,
            pl.BlockSpec((rows, 128), lambda i: (i + part * steps, 1)),
            block,
            block,
            pl.BlockSpec(q_all.shape, lambda i: (0, 0, 0)),
            pl.BlockSpec(g_all.shape, lambda i: (0, 0, 0)),
        ],
        out_specs=[pl.BlockSpec((rows, 128), lambda i: (i, 0))] * 2,
        out_shape=[jax.ShapeDtypeStruct((total, 128), BF16)] * 2,
        cost_estimate=pl.CostEstimate(
            flops=total * slab * 256 * 8,
            transcendentals=total * slab * 2,
            bytes_accessed=total * 2048 + slab * 512,
        ),
        name="attend_dkv",
    )(kv, kv, cos, sin, q_all, g_all)


def mlp_grads_kernel(down, at_ref, *refs):
    mine_ref, other_ref, w_ref = refs[:3]
    outs = refs[-3:] if down % 128 == 0 else refs[-2:]
    data = jnp.where(pl.program_id(0) == 0, mine_ref[...], other_ref[...])
    rows = outs[0].shape[0]
    nf = (data.shape[0] - down) // (2 * rows)
    ff = outs[0].shape[1] // (2 * nf)
    for f in range(nf):
        for g in range(2):
            first = (2 * f + g) * rows
            column = (g * nf + f) * ff
            outs[0][:, column : column + ff] = data[first : first + rows, :ff].astype(F32)
    product = outs[0][...] * w_ref[...].astype(F32)
    total = jnp.sum(product, axis=1, keepdims=True)
    outs[1][...] = jnp.broadcast_to(total, outs[1].shape)
    if down % 128 == 0:
        outs[2][...] = data[2 * nf * rows :, :].astype(F32).T[:ff, :]


def mlp_grads_call(at, mine, other, w_in, done, chunks, columns, ff):
    rows = w_in.shape[0] // chunks
    whole = pl.BlockSpec(mine.shape, lambda i, at: (0, 0))
    specs = [
        pl.BlockSpec((rows, w_in.shape[1]), lambda i, at: (at[i], 0)),
        pl.BlockSpec((rows, 128), lambda i, at: (at[i], 0)),
    ]
    shapes = [
        jax.ShapeDtypeStruct(w_in.shape, F32),
        jax.ShapeDtypeStruct((w_in.shape[0], 128), F32),
    ]
    if columns % 128 == 0:
        specs.append(pl.BlockSpec((ff, columns), lambda i, at: (0, at[i])))
        shapes.append(jax.ShapeDtypeStruct((ff, columns * chunks), F32))
    return pl.pallas_call(
        functools.partial(mlp_grads_kernel, columns),
        grid_spec=pltpu.PrefetchScalarGridSpec(
            num_scalar_prefetch=1,
            grid=(2,),
            in_specs=[whole, whole, specs[0]] + [pl.BlockSpec(memory_space=pl.ANY)] * len(done),
            out_specs=specs,
        ),
        out_shape=shapes,
        input_output_aliases={4 + i: i for i in range(len(done))},
        name="mlp_grads",
    )(at, mine, other, w_in, *done)


def attn_grads_kernel(in_ref, w_ref, dqkv_ref, gain_ref, dout_ref):
    lo, rows = in_ref.shape[1], dqkv_ref.shape[0]
    blocks = dqkv_ref.shape[1] // 128
    nf = blocks // (3 * lo)
    total = jnp.zeros((rows, 1), F32)
    for j in range(3):
        for f in range(nf):
            for l in range(lo):
                first = (f * 3 + j) * rows
                at = (j * nf * lo + f * lo + l) * 128
                piece = in_ref[0, l, first : first + rows, :].astype(F32)
                dqkv_ref[:, at : at + 128] = piece
                weights = w_ref[:, at : at + 128].astype(F32)
                total = total + jnp.sum(piece * weights, axis=1, keepdims=True)
    gain_ref[...] = jnp.broadcast_to(total, gain_ref.shape)
    base, some = nf * 3 * rows, dout_ref.shape[1]
    for l in range(lo):
        for b in range(dout_ref.shape[2] // 128):
            first = base + b * some
            dout_ref[l, :, b * 128 : b * 128 + 128] = in_ref[0, l, first : first + some, :].astype(F32)


def attn_grads_call(gathered, w_qkv, width):
    hi, lo = gathered.shape[:2]
    per, columns = w_qkv.shape
    rows, some = per // hi, per // hi // lo
    outs = pl.pallas_call(
        attn_grads_kernel,
        grid=(hi,),
        in_specs=[
            pl.BlockSpec((1,) + gathered.shape[1:], lambda i: (i, 0, 0, 0)),
            pl.BlockSpec((rows, columns), lambda i: (i, 0)),
        ],
        out_specs=[
            pl.BlockSpec((rows, columns), lambda i: (i, 0)),
            pl.BlockSpec((rows, 128), lambda i: (i, 0)),
            pl.BlockSpec((lo, some, width), lambda i: (0, i, 0)),
        ],
        out_shape=[
            jax.ShapeDtypeStruct((per, columns), F32),
            jax.ShapeDtypeStruct((per, 128), F32),
            jax.ShapeDtypeStruct((lo, per // lo, width), F32),
        ],
        name="attn_grads",
    )(gathered, w_qkv)
    return outs[0], outs[1][:, 0], outs[2].reshape(per, width)


def gelu_parts(inner):
    phi = 0.5 * (1.0 + lax.erf(inner * SQRT_HALF))
    slope = phi + inner * jnp.exp(-0.5 * inner * inner) * INV_SQRT_TAU
    return inner * phi, slope


def exchange(parts, axes):
    return lax.all_to_all(parts, axes, 0, 0, tiled=True)


def swap_lo(values):
    return lax.ppermute(values, "lo", [(0, 1), (1, 0)])


def pick(values, axis, index):
    return lax.dynamic_index_in_dim(values, index, axis, keepdims=False)


def fence(*values):
    return lax.optimization_barrier(values)


def on_device(x, gain_attn, w_qkv, w_out, gain_mlp, w_in, w_down, cotangent):
    lo, nf, hi = lax.axis_size("lo"), lax.axis_size("fsdp"), lax.axis_size("hi")
    rows, width = x.shape
    slab = rows * lo * nf
    here = lax.axis_index("lo")
    ff = w_down.shape[0]
    wide = -(-ff // 128) * 128
    w_down = jnp.pad(w_down, ((0, wide - ff), (0, 0)))

    x_slab = lax.all_gather(x, SLAB, axis=0, tiled=True)
    gains = lax.all_gather(jnp.stack([gain_attn, gain_mlp]), "fsdp", axis=1, tiled=True)
    gain_one, gain_two = gains[:1].astype(F32), gains[1:].astype(F32)
    wq = pick(w_qkv.reshape(-1, 3, nf, lo, 128), 3, here)
    wq = wq.transpose(2, 0, 1, 3).reshape(nf, -1, 384)
    wq = exchange(wq, "fsdp").reshape(width, 384)
    out_full = lax.all_gather(w_out, "fsdp", axis=0, tiled=True)
    wi = w_in.reshape(-1, 2, nf, ff).transpose(2, 1, 0, 3)

    first = lax.axis_index("hi") * slab
    half = HD // 2
    freq = THETA ** (-((jnp.arange(128) % half).astype(F32) * 2.0 / HD))
    angle = (first + jnp.arange(slab)).astype(F32)[:, None] * freq[None, :]
    cos, sin = jnp.cos(angle), jnp.sin(angle)

    wq, wi, cos, sin = fence(wq, wi, cos, sin)
    xn1_slab, q, kv = qkv_call(x_slab, gain_one, wq, cos, sin)
    kv, wi = fence(kv, wi)
    wi = exchange(wi, "fsdp")
    ct_all = lax.all_gather(cotangent, "fsdp", axis=0, tiled=True)
    ring = [(i, (i + 1) % hi) for i in range(hi)]
    kvs, state = [kv], ()
    for i in range(hi):
        last = i == hi - 1
        if last:
            q, wi = lax.optimization_barrier((q, wi))
        else:
            after = lax.ppermute(kvs[i], "hi", ring)
        state = attend_call(q, kvs[i], state, last)
        if not last:
            after, state = fence(after, state)
            kvs.append(after)
        if i == 1:
            out_full, ct_all, q = fence(out_full, ct_all, q)
    o, lse = state
    w_a, w_b = [
        jnp.pad(wi[:, g].reshape(width, ff), ((0, 0), (0, wide - ff))) for g in range(2)
    ]

    q_pack = pack_call(pack_q_kernel, q, lse, 3, "pack_q")
    q_all = lax.all_gather(q_pack, "hi", axis=0)

    o_own = exchange(o.reshape(lo * nf, rows, 128), SLAB)
    o_own = o_own.reshape(lo, nf, rows, 128).transpose(2, 1, 0, 3).reshape(rows, width)
    xf = x.astype(F32)
    hidden = xf + nn_dot(o_own, out_full)
    xn2, n2, r2 = layer_norm(hidden, gain_two)
    xn2_all = lax.all_gather(xn2.astype(BF16), "fsdp", axis=0, tiled=True)

    a, b = nn_dot(xn2_all, w_a), nn_dot(xn2_all, w_b)
    act, slope = gelu_parts(a)
    u = (act * b).astype(BF16)
    du = nt_dot(ct_all, w_down)
    da = (du * b * slope).astype(BF16)
    db = (du * act).astype(BF16)

    d_xn2 = (nt_dot(da, w_a) + nt_dot(db, w_b)).astype(BF16).reshape(nf, rows, width)
    d_xn2 = jnp.sum(exchange(d_xn2, "fsdp").astype(F32), axis=0)
    d_hidden = cotangent.astype(F32) + norm_back(d_xn2, n2, r2, gain_two)
    dhb = d_hidden.astype(BF16)
    d_o = nt_dot(dhb, out_full).astype(BF16)
    d_o = d_o.reshape(rows, nf, lo, 128).transpose(2, 1, 0, 3).reshape(lo * nf, rows, 128)
    grads = exchange(d_o, SLAB).reshape(slab, 128)


    per, chunks = width // nf, lo * hi
    p_in = jnp.stack([tn_dot(xn2_all, da), tn_dot(xn2_all, db)], axis=1).astype(BF16)
    p_in = p_in.reshape(nf, chunks, per // chunks, 2, wide).transpose(1, 0, 3, 2, 4)
    p_down = tn_dot(ct_all, u).astype(BF16).reshape(chunks, -1, wide)
    parts = jnp.concatenate([p_in.reshape(chunks, -1, wide), p_down], axis=1)

    at_hi = lax.axis_index("hi")

    def own(member, step):
        return pick(parts, 0, member * hi + (at_hi - 1 - step) % hi)

    def summed(step, *arrived):
        total = own(here, step).astype(F32)
        for piece in arrived:
            total = total + piece.astype(F32)
        return total.astype(BF16)

    from_lo = swap_lo(own(1 - here, 0))
    parts, grads = fence(parts, grads)
    g_pack = pack_call(pack_g_kernel, grads, o, 2, "pack_g")
    g_all = lax.all_gather(g_pack, "hi", axis=0)
    dhb, g_pack = fence(dhb, g_pack)
    dhb_slab = lax.all_gather(dhb, SLAB, axis=0, tiled=True)

    halves = 2
    dqs, dkvs = [], []

    def work(step):
        if step < halves:
            dqs.append(dq_call(q, grads, o, lse, cos, sin, kvs, step, halves))
        elif step < 2 * halves:
            dkvs.append(dkv_call(kv, cos, sin, q_all, g_all, step - halves, halves))

    def fence_with_work(step, *values):
        held = dqs if step < halves else dkvs
        out = fence(*values, held[-1])
        held[-1] = out[-1]
        return out[:-1]

    from_hi = ()
    for step in range(hi - 1):
        to_hi = summed(step, from_lo, *from_hi)
        from_hi = lax.ppermute(to_hi, "hi", ring)
        from_lo = swap_lo(own(1 - here, step + 1))
        work(step)
        if step < 2 * halves:
            from_hi, from_lo, parts = fence_with_work(step, from_hi, from_lo, parts)
        from_hi = (from_hi,)
    parts, u = fence(parts, u)
    mine = summed(hi - 1, from_lo, *from_hi)
    split = 2 * nf * (per // chunks)
    turned = exchange(mine[:split].reshape(nf, -1, wide), "fsdp").reshape(split, wide)
    for step in range(hi - 1, 2 * halves):
        work(step)
    dqkv = jnp.concatenate(
        [jnp.concatenate(dqs), jnp.concatenate([d[0] for d in dkvs]), jnp.concatenate([d[1] for d in dkvs])],
        axis=1,
    )
    mine = jnp.concatenate([turned, mine[split:]], axis=0)
    mine, dqkv = fence(mine, dqkv)

    done = ()
    downs = jnp.zeros((chunks, width // chunks, wide), BF16)

    def spread(step, chunk, done, downs):
        other = swap_lo(chunk)
        after = lax.ppermute(chunk, "hi", ring) if step < hi - 1 else None
        return other, after

    def place(step, chunk, other, done, downs):
        at = (at_hi - step) % hi
        at = jnp.stack([here * hi + at, (1 - here) * hi + at])
        done = mlp_grads_call(at, chunk, other, w_in, done, chunks, width // chunks, ff)
        if len(done) == 2:
            for index, piece in ((at[0], chunk), (at[1], other)):
                downs = lax.dynamic_update_index_in_dim(downs, piece[split:], index, 0)
        return done, downs

    other, after = spread(0, mine, done, downs)

    p_qkv = tn_dot(xn1_slab, dqkv).astype(BF16)
    p_qkv = p_qkv.reshape(nf, hi, per // hi, 3, 128).transpose(1, 0, 3, 2, 4)
    p_qkv = exchange(p_qkv.reshape(hi * nf, 3, per // hi, 128), ("hi", "fsdp"))
    d_xn1 = nt_dot(dqkv, wq).astype(BF16).reshape(lo * nf, rows, width)
    d_xn1 = exchange(d_xn1, SLAB)
    p_out = exchange(tn_dot(o, dhb_slab).astype(BF16).reshape(hi, -1, width), "hi")
    p_out = jnp.sum(p_out.astype(F32), axis=0).astype(BF16)
    p_out = p_out.reshape(-1, width // 128, 128).transpose(1, 0, 2).reshape(-1, 128)
    p_qkv = jnp.sum(p_qkv.reshape(hi, -1, 128).astype(F32), axis=0).astype(BF16)
    gathered = lax.all_gather(jnp.concatenate([p_qkv, p_out], axis=0), ("hi", "lo"), axis=0)
    gathered = gathered.reshape((hi, lo) + gathered.shape[1:])

    chunk = mine
    for step in range(hi):
        done, downs = place(step, chunk, other, done, downs)
        if step < hi - 1:
            chunk = after
            other, after = spread(step + 1, chunk, done, downs)
    if len(done) == 3:
        d_w_down = done[2]
    else:
        d_w_down = downs.reshape(width, wide)[:, :ff].T.astype(F32)
    d_w_in = done[0]
    d_w_qkv, gain_sum, d_w_out = attn_grads_call(gathered, w_qkv, width)

    out_part = nn_dot(u, w_down).astype(BF16).reshape(nf, rows, width)
    out_sum = jnp.sum(exchange(out_part, "fsdp").astype(F32), axis=0)
    output = (hidden + out_sum).astype(BF16)

    d_xn1 = jnp.sum(d_xn1.astype(F32), axis=0)
    _, n1, r1 = layer_norm(xf, gain_one)
    d_x = d_hidden + norm_back(d_xn1, n1, r1, gain_one)

    d_gain_attn = gain_sum / gain_attn.astype(F32)
    d_gain_mlp = done[1][:, 0] / gain_mlp.astype(F32)
    return (output, d_x, d_gain_attn, d_gain_mlp, d_w_qkv, d_w_out, d_w_in, d_w_down)


def solution(mesh):
    ctx, fsdp = mesh.shape["ctx"], mesh.shape["fsdp"]
    lo = H // 2 // fsdp
    split = Mesh(mesh.devices.reshape(ctx // lo, lo, fsdp), ("hi", "lo", "fsdp"))
    tokens = P(("hi", "lo", "fsdp"), None)
    shards = P("fsdp", None)
    return jax.shard_map(
        on_device,
        mesh=split,
        in_specs=(tokens, P("fsdp"), shards, shards, P("fsdp"), shards, shards, tokens),
        out_specs=(tokens, tokens, P("fsdp"), P("fsdp"), shards, shards, shards, shards),
        check_vma=False,
    )
```

```python
import functools

import jax
import jax.numpy as jnp
from jax import lax
from jax.experimental import pallas as pl
from jax.experimental.pallas import tpu as pltpu
from jax.sharding import Mesh, PartitionSpec as P


H = 16
HD = 64
EPS = 1e-05
THETA = 160000.0
SQRT_HALF = 0.7071067811865476
INV_SQRT_TAU = 0.3989422804014327
LOG2E = 1.4426950408889634
SCALE = 0.125
C2 = SCALE * LOG2E
F32 = jnp.float32
BF16 = jnp.bfloat16
SLAB = ("lo", "fsdp")


def nt_dot(a, b):
    return lax.dot_general(a, b, (((1,), (1,)), ((), ())), preferred_element_type=F32)


def tn_dot(a, b):
    return lax.dot_general(a, b, (((0,), (0,)), ((), ())), preferred_element_type=F32)


def nn_dot(a, b):
    return jnp.dot(a, b, preferred_element_type=F32)


def layer_norm(values, gain):
    middle = jnp.mean(values, axis=-1, keepdims=True)
    centered = values - middle
    spread = jnp.mean(centered * centered, axis=-1, keepdims=True)
    inverse = lax.rsqrt(spread + EPS)
    normed = centered * inverse
    return (normed * gain, normed, inverse)


def norm_back(incoming, normed, inverse, gain):
    scaled = incoming * gain
    return inverse * (
        scaled
        - jnp.mean(scaled, axis=-1, keepdims=True)
        - normed * jnp.mean(scaled * normed, axis=-1, keepdims=True)
    )


def half_turn(u):
    lane = lax.broadcasted_iota(jnp.int32, u.shape, 1)
    return jnp.where(lane % HD < HD // 2, -pltpu.roll(u, 96, 1), pltpu.roll(u, 32, 1))


def lanes_of(values, head):
    lane = lax.broadcasted_iota(jnp.int32, values.shape, 1)
    return jnp.where((lane >= HD) == (head == 1), values, jnp.zeros_like(values))


def merge(first, second):
    shape = first.shape if first.shape[1] > 1 else (first.shape[0], 128)
    lane = lax.broadcasted_iota(jnp.int32, shape, 1)
    return jnp.where(lane < HD, first, second)


def qkv_kernel(x_ref, g_ref, w_ref, cos_ref, sin_ref, xn_ref, q_ref, kv_ref):
    xn, _, _ = layer_norm(x_ref[...].astype(F32), g_ref[...])
    xnb = xn.astype(BF16)
    xn_ref[...] = xnb
    out = nn_dot(xnb, w_ref[...])
    cos, sin = cos_ref[...], sin_ref[...]
    q, k = out[:, :128], out[:, 128:256]
    q_ref[...] = (q * cos + half_turn(q) * sin).astype(BF16)
    kv_ref[:, :128] = (k * cos + half_turn(k) * sin).astype(BF16)
    kv_ref[:, 128:] = out[:, 256:].astype(BF16)


def qkv_call(x, gain, w, cos, sin, rows=256):
    total, width = x.shape
    return pl.pallas_call(
        qkv_kernel,
        grid=(total // rows,),
        in_specs=[
            pl.BlockSpec((rows, width), lambda i: (i, 0)),
            pl.BlockSpec((1, width), lambda i: (0, 0)),
            pl.BlockSpec(w.shape, lambda i: (0, 0)),
            pl.BlockSpec((rows, 128), lambda i: (i, 0)),
            pl.BlockSpec((rows, 128), lambda i: (i, 0)),
        ],
        out_specs=[
            pl.BlockSpec((rows, width), lambda i: (i, 0)),
            pl.BlockSpec((rows, 128), lambda i: (i, 0)),
            pl.BlockSpec((rows, 256), lambda i: (i, 0)),
        ],
        out_shape=[
            jax.ShapeDtypeStruct((total, width), BF16),
            jax.ShapeDtypeStruct((total, 128), BF16),
            jax.ShapeDtypeStruct((total, 256), BF16),
        ],
        name="qkv_rope",
    )(x, gain, w, cos, sin)


def attend_kernel(begin, end, q_ref, k_ref, v_ref, *refs):
    q, k, v = q_ref[...], k_ref[...], v_ref[...]
    if not begin:
        tops, masses, acc = [r[...] for r in refs[:3]]
    new = []
    for h in range(2):
        s = nt_dot(lanes_of(q, h), k)
        top = jnp.max(s, axis=1, keepdims=True)
        if not begin:
            old = tops[:, h * HD : h * HD + 1]
            top = jnp.maximum(old, top)
            keep = jnp.exp2((old - top) * C2)
        p = jnp.exp2((s - top) * C2)
        mass = jnp.sum(p, axis=1, keepdims=True)
        part = nn_dot(p.astype(BF16), v)
        if not begin:
            mass = mass + masses[:, h * HD : h * HD + 1] * keep
            part = part + acc * keep
        new.append((top, mass, part))
    if end:
        refs[-2][...] = merge(*[part / mass for _, mass, part in new]).astype(BF16)
        refs[-1][...] = merge(*[top * C2 + jnp.log2(mass) for top, mass, _ in new])
    else:
        for ref, both in zip(refs[-3:], zip(*new)):
            ref[...] = merge(*both)


def attend_call(q, kv, state, end, rows=256):
    total, keys = q.shape[0], kv.shape[0]
    block = pl.BlockSpec((rows, 128), lambda i: (i, 0))
    shapes = [BF16, F32] if end else [F32] * 3
    work = total * keys * 256 * 4
    return pl.pallas_call(
        functools.partial(attend_kernel, not state, end),
        grid=(total // rows,),
        in_specs=[
            block,
            pl.BlockSpec((keys, 128), lambda i: (0, 0)),
            pl.BlockSpec((keys, 128), lambda i: (0, 1)),
        ]
        + [block] * len(state),
        out_specs=[block] * len(shapes),
        out_shape=[jax.ShapeDtypeStruct((total, 128), t) for t in shapes],
        cost_estimate=pl.CostEstimate(
            flops=work, transcendentals=total * keys * 2, bytes_accessed=total * 4096
        ),
        name="attend",
    )(q, kv, kv, *state)


def column_to_rows(values, parts):
    blocks = values.shape[0] // 128
    flipped = [values[b * 128 : (b + 1) * 128, :].T for b in range(blocks)]
    rows = []
    for h in range(2):
        left = jnp.concatenate([f[h * HD : h * HD + 1, :] for f in flipped], axis=0)
        for _ in range(parts):
            piece = left.astype(BF16)
            rows.append(piece.astype(F32))
            left = left - piece.astype(F32)
    return jnp.concatenate(rows, axis=0).astype(BF16)


def pack_q_kernel(q_ref, lse_ref, out_ref):
    total = q_ref.shape[0]
    out_ref[:total, :] = q_ref[...]
    out_ref[total:, :] = column_to_rows(lse_ref[...], 3)


def pack_g_kernel(g_ref, o_ref, out_ref):
    total = g_ref.shape[0]
    g = g_ref[...]
    out_ref[:total, :] = g
    prod = g.astype(F32) * o_ref[...].astype(F32)
    sums = [jnp.sum(lanes_of(prod, h), axis=1, keepdims=True) for h in range(2)]
    out_ref[total:, :] = column_to_rows(merge(*sums), 2)


def pack_call(kernel, first, second, parts):
    total = first.shape[0]
    return pl.pallas_call(
        kernel, out_shape=jax.ShapeDtypeStruct((total + total // 128 * 2 * parts, 128), BF16)
    )(first, second)


def dq_kernel(chunks, q_ref, g_ref, o_ref, lse_ref, cos_ref, sin_ref, *refs):
    q, g = q_ref[...], g_ref[...]
    prod = g.astype(F32) * o_ref[...].astype(F32)
    lse = lse_ref[...]
    done = []
    for h in range(2):
        qh, gh = lanes_of(q, h), lanes_of(g, h)
        delta = jnp.sum(lanes_of(prod, h), axis=1, keepdims=True)
        total = jnp.zeros(q.shape, F32)
        for kv_ref in refs[:chunks]:
            k, v = kv_ref[:, :128], kv_ref[:, 128:]
            p = jnp.exp2(nt_dot(qh, k) * C2 - lse[:, h * HD : h * HD + 1])
            ds = (p * (nt_dot(gh, v) - delta)).astype(BF16)
            total = total + nn_dot(ds, k)
        done.append(total)
    dq = merge(*done) * SCALE
    refs[-1][...] = (dq * cos_ref[...] - half_turn(dq) * sin_ref[...]).astype(BF16)


def dq_call(q, g, o, lse, cos, sin, kvs, part, parts, done, rows=256):
    total, keys = q.shape[0] // parts, kvs[0].shape[0]
    steps = total // rows
    block = pl.BlockSpec((rows, 128), lambda i: (i + part * steps, 0))
    return pl.pallas_call(
        functools.partial(dq_kernel, len(kvs)),
        grid=(steps,),
        in_specs=[block] * 6
        + [pl.BlockSpec((keys, 256), lambda i: (0, 0))] * len(kvs)
        + [pl.BlockSpec(memory_space=pl.ANY)] * len(done),
        out_specs=[block],
        out_shape=[jax.ShapeDtypeStruct(q.shape, BF16)],
        input_output_aliases={6 + len(kvs) + i: i for i in range(len(done))},
        cost_estimate=pl.CostEstimate(
            flops=total * keys * len(kvs) * 256 * 6,
            transcendentals=total * keys * len(kvs) * 2,
            bytes_accessed=total * 2048 + keys * len(kvs) * 512,
        ),
        name="attend_dq",
    )(q, g, o, lse, cos, sin, *kvs, *done)


def row_of(stats, head, parts, blocks):
    base = head * parts * blocks
    pieces = [stats[base + i * blocks : base + (i + 1) * blocks, :].astype(F32) for i in range(parts)]
    whole = functools.reduce(lambda a, b: a + b, pieces)
    return jnp.concatenate([whole[b : b + 1, :] for b in range(blocks)], axis=1)


def dkv_kernel(k_ref, v_ref, cos_ref, sin_ref, q_ref, g_ref, *refs):
    dk_ref, dv_ref = refs[-2:]
    k, v = k_ref[...], v_ref[...]
    rows = k.shape[0]
    ks = [lanes_of(k, h) for h in range(2)]
    vs = [lanes_of(v, h) for h in range(2)]
    blocks = (q_ref.shape[1] - g_ref.shape[1]) // 2
    slab = blocks * 128

    def step(j, carry):
        q = q_ref[j, :slab, :]
        g = g_ref[j, :slab, :]
        lse = q_ref[j, slab:, :].astype(F32)
        delta = g_ref[j, slab:, :].astype(F32)
        new = []
        for h in range(2):
            dk, dv = carry[h]
            p = jnp.exp2(nt_dot(ks[h], q) * C2 - row_of(lse, h, 3, blocks))
            ds = (p * (nt_dot(vs[h], g) - row_of(delta, h, 2, blocks))).astype(BF16)
            dv = dv + nn_dot(p.astype(BF16), g)
            dk = dk + nn_dot(ds, q)
            new.append((dk, dv))
        return tuple(new)

    zero = jnp.zeros((rows, 128), F32)
    done = lax.fori_loop(0, q_ref.shape[0], step, ((zero, zero), (zero, zero)))
    dk = merge(done[0][0], done[1][0]) * SCALE
    dk_ref[...] = (dk * cos_ref[...] - half_turn(dk) * sin_ref[...]).astype(BF16)
    dv_ref[...] = merge(done[0][1], done[1][1]).astype(BF16)


def dkv_call(kv, cos, sin, q_all, g_all, part, parts, done, rows=256):
    total = kv.shape[0] // parts
    slab = kv.shape[0] * q_all.shape[0]
    steps = total // rows
    block = pl.BlockSpec((rows, 128), lambda i: (i + part * steps, 0))
    return pl.pallas_call(
        dkv_kernel,
        grid=(steps,),
        in_specs=[
            block,
            pl.BlockSpec((rows, 128), lambda i: (i + part * steps, 1)),
            block,
            block,
            pl.BlockSpec(q_all.shape, lambda i: (0, 0, 0)),
            pl.BlockSpec(g_all.shape, lambda i: (0, 0, 0)),
        ]
        + [pl.BlockSpec(memory_space=pl.ANY)] * len(done),
        out_specs=[block] * 2,
        out_shape=[jax.ShapeDtypeStruct((kv.shape[0], 128), BF16)] * 2,
        input_output_aliases={6 + i: i for i in range(len(done))},
        cost_estimate=pl.CostEstimate(
            flops=total * slab * 256 * 8,
            transcendentals=total * slab * 2,
            bytes_accessed=total * 2048 + slab * 512,
        ),
        name="attend_dkv",
    )(kv, kv, cos, sin, q_all, g_all, *done)


def mlp_grads_kernel(down, at_ref, *refs):
    mine_ref, other_ref, w_ref = refs[:3]
    outs = refs[-3:] if down % 128 == 0 else refs[-2:]
    data = jnp.where(pl.program_id(0) == 0, mine_ref[...], other_ref[...])
    rows = outs[0].shape[0]
    nf = (data.shape[0] - down) // (2 * rows)
    ff = outs[0].shape[1] // (2 * nf)
    for f in range(nf):
        for g in range(2):
            first = (2 * f + g) * rows
            column = (g * nf + f) * ff
            outs[0][:, column : column + ff] = data[first : first + rows, :ff].astype(F32)
    product = outs[0][...] * w_ref[...].astype(F32)
    total = jnp.sum(product, axis=1, keepdims=True)
    outs[1][...] = jnp.broadcast_to(total, outs[1].shape)
    if down % 128 == 0:
        outs[2][...] = data[2 * nf * rows :, :].astype(F32).T[:ff, :]


def mlp_grads_call(at, mine, other, w_in, done, chunks, columns, ff):
    rows = w_in.shape[0] // chunks
    whole = pl.BlockSpec(mine.shape, lambda i, at: (0, 0))
    specs = [
        pl.BlockSpec((rows, w_in.shape[1]), lambda i, at: (at[i], 0)),
        pl.BlockSpec((rows, 128), lambda i, at: (at[i], 0)),
    ]
    shapes = [
        jax.ShapeDtypeStruct(w_in.shape, F32),
        jax.ShapeDtypeStruct((w_in.shape[0], 128), F32),
    ]
    if columns % 128 == 0:
        specs.append(pl.BlockSpec((ff, columns), lambda i, at: (0, at[i])))
        shapes.append(jax.ShapeDtypeStruct((ff, columns * chunks), F32))
    return pl.pallas_call(
        functools.partial(mlp_grads_kernel, columns),
        grid_spec=pltpu.PrefetchScalarGridSpec(
            num_scalar_prefetch=1,
            grid=(2,),
            in_specs=[whole, whole, specs[0]] + [pl.BlockSpec(memory_space=pl.ANY)] * len(done),
            out_specs=specs,
        ),
        out_shape=shapes,
        input_output_aliases={4 + i: i for i in range(len(done))},
        name="mlp_grads",
    )(at, mine, other, w_in, *done)


def attn_grads_kernel(at_ref, mine_ref, other_ref, w_ref, *refs):
    dqkv_ref, gain_ref, dout_ref = refs[-3:]
    rows, lo = dqkv_ref.shape[0], dout_ref.shape[0]
    nf = dqkv_ref.shape[1] // (3 * lo * 128)
    swapped = at_ref[1] == 1
    data = [
        jnp.where(swapped, other_ref[...], mine_ref[...]),
        jnp.where(swapped, mine_ref[...], other_ref[...]),
    ]
    total = jnp.zeros((rows, 1), F32)
    for j in range(3):
        for f in range(nf):
            first = (f * 3 + j) * rows
            for l in range(lo):
                at = (j * nf * lo + f * lo + l) * 128
                piece = data[l][first : first + rows, :].astype(F32)
                dqkv_ref[:, at : at + 128] = piece
                weights = w_ref[:, at : at + 128].astype(F32)
                total = total + jnp.sum(piece * weights, axis=1, keepdims=True)
    gain_ref[...] = jnp.broadcast_to(total, gain_ref.shape)
    base, some = nf * 3 * rows, dout_ref.shape[1]
    for l in range(lo):
        for b in range(dout_ref.shape[2] // 128):
            first = base + b * some
            piece = data[l][first : first + some, :].astype(F32)
            dout_ref[l, :, b * 128 : b * 128 + 128] = piece


def attn_grads_call(at, mine, other, w_qkv, done, hi, lo, width):
    per, columns = w_qkv.shape
    rows, some = per // hi, per // hi // lo
    whole = pl.BlockSpec(mine.shape, lambda i, at: (0, 0))
    return pl.pallas_call(
        attn_grads_kernel,
        grid_spec=pltpu.PrefetchScalarGridSpec(
            num_scalar_prefetch=1,
            grid=(1,),
            in_specs=[whole, whole, pl.BlockSpec((rows, columns), lambda i, at: (at[0], 0))]
            + [pl.BlockSpec(memory_space=pl.ANY)] * len(done),
            out_specs=[
                pl.BlockSpec((rows, columns), lambda i, at: (at[0], 0)),
                pl.BlockSpec((rows, 128), lambda i, at: (at[0], 0)),
                pl.BlockSpec((lo, some, width), lambda i, at: (0, at[0], 0)),
            ],
        ),
        out_shape=[
            jax.ShapeDtypeStruct((per, columns), F32),
            jax.ShapeDtypeStruct((per, 128), F32),
            jax.ShapeDtypeStruct((lo, per // lo, width), F32),
        ],
        input_output_aliases={4 + i: i for i in range(len(done))},
        name="attn_grads",
    )(at, mine, other, w_qkv, *done)


def gelu_parts(inner):
    phi = 0.5 * (1.0 + lax.erf(inner * SQRT_HALF))
    slope = phi + inner * jnp.exp(-0.5 * inner * inner) * INV_SQRT_TAU
    return inner * phi, slope


def exchange(parts, axes):
    return lax.all_to_all(parts, axes, 0, 0, tiled=True)


def swap_lo(values):
    return lax.ppermute(values, "lo", [(0, 1), (1, 0)])


def pick(values, axis, index):
    return lax.dynamic_index_in_dim(values, index, axis, keepdims=False)


def fence(*values):
    return lax.optimization_barrier(values)


def on_device(x, gain_attn, w_qkv, w_out, gain_mlp, w_in, w_down, cotangent):
    lo, nf, hi = lax.axis_size("lo"), lax.axis_size("fsdp"), lax.axis_size("hi")
    rows, width = x.shape
    slab = rows * lo * nf
    here = lax.axis_index("lo")
    ff = w_down.shape[0]
    wide = -(-ff // 128) * 128
    w_down = jnp.pad(w_down, ((0, wide - ff), (0, 0)))

    x_slab = lax.all_gather(x, SLAB, axis=0, tiled=True)
    gains = lax.all_gather(jnp.stack([gain_attn, gain_mlp]), "fsdp", axis=1, tiled=True)
    gain_one, gain_two = gains[:1].astype(F32), gains[1:].astype(F32)
    wq = pick(w_qkv.reshape(-1, 3, nf, lo, 128), 3, here)
    wq = wq.transpose(2, 0, 1, 3).reshape(nf, -1, 384)
    wq = exchange(wq, "fsdp").reshape(width, 384)
    out_full = lax.all_gather(w_out, "fsdp", axis=0, tiled=True)
    wi = w_in.reshape(-1, 2, nf, ff).transpose(2, 1, 0, 3)

    first = lax.axis_index("hi") * slab
    half = HD // 2
    freq = THETA ** (-((jnp.arange(128) % half).astype(F32) * 2.0 / HD))
    angle = (first + jnp.arange(slab)).astype(F32)[:, None] * freq[None, :]
    cos, sin = jnp.cos(angle), jnp.sin(angle)

    wq, wi, cos, sin = fence(wq, wi, cos, sin)
    xn1_slab, q, kv = qkv_call(x_slab, gain_one, wq, cos, sin)
    ct_all = lax.all_gather(cotangent, "fsdp", axis=0, tiled=True)
    ring = [(i, (i + 1) % hi) for i in range(hi)]
    kvs, state = [kv], ()
    for i in range(hi):
        last = i == hi - 1
        if not last:
            after = lax.ppermute(kvs[i], "hi", ring)
        else:
            q, wi = fence(q, wi)
        state = attend_call(q, kvs[i], state, last)
        if i == 0:
            state, wi = fence(state, wi)
            wi = exchange(wi, "fsdp")
        if not last:
            after, state = fence(after, state)
            kvs.append(after)
    o, lse = state
    w_a, w_b = [
        jnp.pad(wi[:, g].reshape(width, ff), ((0, 0), (0, wide - ff))) for g in range(2)
    ]

    q_pack = pack_call(pack_q_kernel, q, lse, 3)
    at_hi = lax.axis_index("hi")
    q_all = jnp.zeros((hi,) + q_pack.shape, BF16)
    for step in range(hi):
        q_all = lax.dynamic_update_index_in_dim(q_all, q_pack, (at_hi - step) % hi, 0)
        if step < hi - 1:
            q_pack = lax.ppermute(q_pack, "hi", ring)

    o_pair = o.reshape(lo, nf * rows, 128)
    o_mine, o_other = pick(o_pair, 0, here), swap_lo(pick(o_pair, 0, 1 - here))
    o_four = jnp.concatenate(
        [jnp.where(here == 0, o_mine, o_other), jnp.where(here == 0, o_other, o_mine)], axis=1
    )

    o_own = exchange(o.reshape(lo * nf, rows, 128), SLAB)
    o_own = o_own.reshape(lo, nf, rows, 128).transpose(2, 1, 0, 3).reshape(rows, width)
    xf = x.astype(F32)
    hidden = xf + nn_dot(o_own, out_full)
    xn2, n2, r2 = layer_norm(hidden, gain_two)
    xn2_all = lax.all_gather(xn2.astype(BF16), "fsdp", axis=0, tiled=True)
    xn2_all, o_four = fence(xn2_all, o_four)

    a, b = nn_dot(xn2_all, w_a), nn_dot(xn2_all, w_b)
    act, slope = gelu_parts(a)
    u = (act * b).astype(BF16)
    du = nt_dot(ct_all, w_down)
    da = (du * b * slope).astype(BF16)
    db = (du * act).astype(BF16)

    per, chunks = width // nf, lo * hi

    def halves(p):
        p = p.reshape((lo, hi) + p.shape[1:])
        return pick(p, 0, here), pick(p, 0, 1 - here)

    def over_hi_scattered(total):
        return lax.psum_scatter(total, "hi", scatter_dimension=0, tiled=True)[0]

    per, chunks = width // nf, lo * hi

    def halves(p):
        p = p.reshape((lo, hi) + p.shape[1:])
        return pick(p, 0, here), pick(p, 0, 1 - here)

    def added(own, other):
        return (own.astype(F32) + other.astype(F32)).astype(BF16)

    def over_hi_scattered(total):
        return lax.psum_scatter(total, "hi", scatter_dimension=0, tiled=True)[0]

    def fold(p, axis, bit):
        mine = lax.axis_index("fsdp") // bit % 2
        other = lax.ppermute(
            pick(p, axis, 1 - mine), "fsdp", [(i, i ^ bit) for i in range(nf)]
        )
        return added(pick(p, axis, mine), other)

    d_xn2 = nt_dot(da, w_a) + nt_dot(db, w_b)
    d_xn2 = fold(d_xn2.astype(BF16).reshape(2, 2, rows, width), 1, 1)
    p_down = halves(tn_dot(ct_all, u).astype(BF16).reshape(chunks, -1, wide))
    mine = lax.axis_index("fsdp") // 2
    d_other = lax.ppermute(pick(d_xn2, 0, 1 - mine), "fsdp", [(i, i ^ 2) for i in range(nf)])
    d_xn2 = pick(d_xn2, 0, mine)
    t_down = swap_lo(p_down[1])
    p_in = jnp.stack([tn_dot(xn2_all, da), tn_dot(xn2_all, db)], axis=1).astype(BF16)
    p_in = p_in.reshape(nf, chunks, per // chunks, 2, wide).transpose(1, 0, 3, 2, 4)
    p_in = halves(p_in.reshape(chunks, -1, wide))
    d_other, p_in = fence(d_other, p_in)

    d_xn2 = d_xn2.astype(F32) + d_other.astype(F32)
    d_hidden = cotangent.astype(F32) + norm_back(d_xn2, n2, r2, gain_two)
    dhb = d_hidden.astype(BF16)
    d_o = nt_dot(dhb, out_full).astype(BF16)
    d_o = d_o.reshape(rows, nf, lo, 128).transpose(2, 1, 0, 3).reshape(lo * nf, rows, 128)
    d_o, own_down = fence(d_o, p_down[0])
    t_down = added(own_down, t_down)
    d_o, t_down = fence(d_o, t_down)

    def down_part(step):
        return pick(t_down, 0, (at_hi - 1 - step) % hi)

    def down_hop(total):
        return lax.ppermute(total, "hi", ring)

    r_down = down_hop(down_part(0))
    dhb_all = lax.all_gather(dhb, "fsdp", axis=0, tiled=True)
    grads = exchange(d_o, SLAB).reshape(slab, 128)
    p_out = halves(tn_dot(o_four, dhb_all).astype(BF16).reshape(chunks, -1, width))
    t_out = swap_lo(p_out[1])
    grads, p_in, q_all, t_down, p_out = fence(grads, p_in, q_all, t_down, p_out)
    t_in = swap_lo(p_in[1])
    g_pack = pack_call(pack_g_kernel, grads, o, 2)
    r_down, g_pack = fence(r_down, g_pack)
    g_all = lax.all_gather(g_pack, "hi", axis=0)
    if hi > 2:
        r_down = down_hop(added(down_part(1), r_down))
    dq = dq_call(q, grads, o, lse, cos, sin, kvs, 0, 1, ())[0]
    u, dq, r_down, t_out = fence(u, dq, r_down, t_out)
    for step in range(2, hi - 1):
        r_down = down_hop(added(down_part(step), r_down))
    t_out = added(p_out[0], t_out)
    out_part = nn_dot(u, w_down).astype(BF16).reshape(nf, rows, width)
    out_part = exchange(out_part, "fsdp")
    g_all, t_out = fence(g_all, t_out)
    r_out = over_hi_scattered(t_out)
    dkv = dkv_call(kv, cos, sin, q_all, g_all, 0, 2, ())
    dkv, t_in, own_in, r_down = fence(dkv, t_in, p_in[0], r_down)
    r_down = added(down_part(hi - 1), r_down)
    t_in = added(own_in, t_in)
    dkv, t_in, r_out = fence(dkv, t_in, r_out)
    r_in = over_hi_scattered(t_in)
    dk, dv = dkv_call(kv, cos, sin, q_all, g_all, 1, 2, dkv)
    dk, out_part = fence(dk, out_part)

    def over_hi(p):
        return jnp.sum(p.reshape(hi, -1, 128).astype(F32), axis=0).astype(BF16)

    dqkv = jnp.concatenate([dq, dk, dv], axis=1)
    p_qkv = tn_dot(xn1_slab, dqkv).astype(BF16)
    p_qkv = p_qkv.reshape(nf, hi, per // hi, 3, 128).transpose(1, 0, 3, 2, 4)
    p_qkv = exchange(p_qkv.reshape(hi * nf, 3, per // hi, 128), ("hi", "fsdp"))
    d_xn1 = nt_dot(dqkv, wq).astype(BF16).reshape(lo, 2, 2, rows, width)
    d_xn1 = fold(d_xn1, 2, 1)
    d_xn1 = fold(d_xn1, 1, 2)
    own_x, other_x = pick(d_xn1, 0, here), swap_lo(pick(d_xn1, 0, 1 - here))
    r_out = r_out.reshape(-1, width // 128, 128).transpose(1, 0, 2).reshape(-1, 128)
    r_in, p_qkv = fence(r_in, p_qkv)
    split = r_in.shape[0]
    r_in = exchange(r_in.reshape(nf, -1, wide), "fsdp").reshape(split, wide)
    mlp = jnp.concatenate([r_in, r_down], axis=0)
    attn = jnp.concatenate([over_hi(p_qkv), r_out], axis=0)

    attn, mlp, own_x, other_x = fence(attn, mlp, own_x, other_x)
    done, placed, downs = (), (), jnp.zeros((chunks, width // chunks, wide), BF16)
    now = (attn, mlp)
    arrived = None

    def place(step, now, others):
        at = (at_hi - step) % hi
        attn_at = jnp.stack([at, here])
        mlp_at = jnp.stack([here * hi + at, (1 - here) * hi + at])
        return (
            attn_grads_call(attn_at, now[0], others[0], w_qkv, placed, hi, lo, width),
            mlp_grads_call(mlp_at, now[1], others[1], w_in, done, chunks, width // chunks, ff),
            mlp_at,
        )

    for step in range(hi + 1):
        others = after = now
        if step < hi:
            others = tuple(swap_lo(p) for p in now)
        if step < hi - 1:
            after = tuple(lax.ppermute(p, "hi", ring) for p in now)
        if arrived:
            placed, done, at = place(step - 1, *arrived)
            if len(done) == 2:
                for index, piece in zip(at, (arrived[0][1], arrived[1][1])):
                    downs = lax.dynamic_update_index_in_dim(downs, piece[split:], index, 0)
        now, others, after, placed, done = fence(now, others, after, placed, done)
        arrived, now = (now, others), after
    if len(done) == 3:
        d_w_down = done[2]
    else:
        d_w_down = downs.reshape(width, wide)[:, :ff].T.astype(F32)
    d_w_in = done[0]
    d_w_qkv, gain_sum, d_w_out = placed[0], placed[1][:, 0], placed[2].reshape(per, width)

    out_sum = jnp.sum(out_part.astype(F32), axis=0)
    output = (hidden + out_sum).astype(BF16)

    d_xn1 = own_x.astype(F32) + other_x.astype(F32)
    _, n1, r1 = layer_norm(xf, gain_one)
    d_x = d_hidden + norm_back(d_xn1, n1, r1, gain_one)

    d_gain_attn = gain_sum / gain_attn.astype(F32)
    d_gain_mlp = done[1][:, 0] / gain_mlp.astype(F32)
    return (output, d_x, d_gain_attn, d_gain_mlp, d_w_qkv, d_w_out, d_w_in, d_w_down)


def solution(mesh):
    ctx, fsdp = mesh.shape["ctx"], mesh.shape["fsdp"]
    lo = H // 2 // fsdp
    split = Mesh(mesh.devices.reshape(ctx // lo, lo, fsdp), ("hi", "lo", "fsdp"))
    tokens = P(("hi", "lo", "fsdp"), None)
    shards = P("fsdp", None)

    return jax.shard_map(
        on_device,
        mesh=split,
        in_specs=(tokens, P("fsdp"), shards, shards, P("fsdp"), shards, shards, tokens),
        out_specs=(tokens, tokens, P("fsdp"), P("fsdp"), shards, shards, shards, shards),
        check_vma=False,
    )
```

```python
import functools

import jax
import jax.numpy as jnp
from jax import lax
from jax.experimental import pallas as pl
from jax.experimental.pallas import tpu as pltpu
from jax.sharding import Mesh, PartitionSpec as P


H = 16
HD = 64
EPS = 1e-05
THETA = 160000.0
SQRT_HALF = 0.7071067811865476
INV_SQRT_TAU = 0.3989422804014327
LOG2E = 1.4426950408889634
SCALE = 0.125
C2 = SCALE * LOG2E
F32 = jnp.float32
BF16 = jnp.bfloat16
SLAB = ("lo", "fsdp")


def nt_dot(a, b):
    return lax.dot_general(a, b, (((1,), (1,)), ((), ())), preferred_element_type=F32)


def tn_dot(a, b):
    return lax.dot_general(a, b, (((0,), (0,)), ((), ())), preferred_element_type=F32)


def nn_dot(a, b):
    return jnp.dot(a, b, preferred_element_type=F32)


def layer_norm(values, gain):
    middle = jnp.mean(values, axis=-1, keepdims=True)
    centered = values - middle
    spread = jnp.mean(centered * centered, axis=-1, keepdims=True)
    inverse = lax.rsqrt(spread + EPS)
    normed = centered * inverse
    return (normed * gain, normed, inverse)


def norm_back(incoming, normed, inverse, gain):
    scaled = incoming * gain
    return inverse * (
        scaled
        - jnp.mean(scaled, axis=-1, keepdims=True)
        - normed * jnp.mean(scaled * normed, axis=-1, keepdims=True)
    )


def half_turn(u):
    lane = lax.broadcasted_iota(jnp.int32, u.shape, 1)
    return jnp.where(lane % HD < HD // 2, -pltpu.roll(u, 96, 1), pltpu.roll(u, 32, 1))


def lanes_of(values, head):
    lane = lax.broadcasted_iota(jnp.int32, values.shape, 1)
    return jnp.where((lane >= HD) == (head == 1), values, jnp.zeros_like(values))


def merge(first, second):
    shape = first.shape if first.shape[1] > 1 else (first.shape[0], 128)
    lane = lax.broadcasted_iota(jnp.int32, shape, 1)
    return jnp.where(lane < HD, first, second)


def qkv_kernel(x_ref, g_ref, w_ref, cos_ref, sin_ref, xn_ref, q_ref, kv_ref):
    xn, _, _ = layer_norm(x_ref[...].astype(F32), g_ref[...])
    xnb = xn.astype(BF16)
    xn_ref[...] = xnb
    out = nn_dot(xnb, w_ref[...])
    cos, sin = cos_ref[...], sin_ref[...]
    q, k = out[:, :128], out[:, 128:256]
    q_ref[...] = (q * cos + half_turn(q) * sin).astype(BF16)
    kv_ref[:, :128] = (k * cos + half_turn(k) * sin).astype(BF16)
    kv_ref[:, 128:] = out[:, 256:].astype(BF16)


def qkv_call(x, gain, w, cos, sin, rows=256):
    total, width = x.shape
    return pl.pallas_call(
        qkv_kernel,
        grid=(total // rows,),
        in_specs=[
            pl.BlockSpec((rows, width), lambda i: (i, 0)),
            pl.BlockSpec((1, width), lambda i: (0, 0)),
            pl.BlockSpec(w.shape, lambda i: (0, 0)),
            pl.BlockSpec((rows, 128), lambda i: (i, 0)),
            pl.BlockSpec((rows, 128), lambda i: (i, 0)),
        ],
        out_specs=[
            pl.BlockSpec((rows, width), lambda i: (i, 0)),
            pl.BlockSpec((rows, 128), lambda i: (i, 0)),
            pl.BlockSpec((rows, 256), lambda i: (i, 0)),
        ],
        out_shape=[
            jax.ShapeDtypeStruct((total, width), BF16),
            jax.ShapeDtypeStruct((total, 128), BF16),
            jax.ShapeDtypeStruct((total, 256), BF16),
        ],
        name="qkv_rope",
    )(x, gain, w, cos, sin)


def attend_kernel(begin, end, q_ref, k_ref, v_ref, *refs):
    q, k, v = q_ref[...], k_ref[...], v_ref[...]
    if not begin:
        tops, masses, acc = [r[...] for r in refs[:3]]
    new = []
    for h in range(2):
        s = nt_dot(lanes_of(q, h), k)
        top = jnp.max(s, axis=1, keepdims=True)
        if not begin:
            old = tops[:, h * HD : h * HD + 1]
            top = jnp.maximum(old, top)
            keep = jnp.exp2((old - top) * C2)
        p = jnp.exp2((s - top) * C2)
        mass = jnp.sum(p, axis=1, keepdims=True)
        part = nn_dot(p.astype(BF16), v)
        if not begin:
            mass = mass + masses[:, h * HD : h * HD + 1] * keep
            part = part + acc * keep
        new.append((top, mass, part))
    if end:
        refs[-2][...] = merge(*[part / mass for _, mass, part in new]).astype(BF16)
        refs[-1][...] = merge(*[top * C2 + jnp.log2(mass) for top, mass, _ in new])
    else:
        for ref, both in zip(refs[-3:], zip(*new)):
            ref[...] = merge(*both)


def attend_call(q, kv, state, end, rows=256):
    total, keys = q.shape[0], kv.shape[0]
    block = pl.BlockSpec((rows, 128), lambda i: (i, 0))
    shapes = [BF16, F32] if end else [F32] * 3
    work = total * keys * 256 * 4
    return pl.pallas_call(
        functools.partial(attend_kernel, not state, end),
        grid=(total // rows,),
        in_specs=[
            block,
            pl.BlockSpec((keys, 128), lambda i: (0, 0)),
            pl.BlockSpec((keys, 128), lambda i: (0, 1)),
        ]
        + [block] * len(state),
        out_specs=[block] * len(shapes),
        out_shape=[jax.ShapeDtypeStruct((total, 128), t) for t in shapes],
        cost_estimate=pl.CostEstimate(
            flops=work, transcendentals=total * keys * 2, bytes_accessed=total * 4096
        ),
        name="attend",
    )(q, kv, kv, *state)


def column_to_rows(values, parts):
    blocks = values.shape[0] // 128
    flipped = [values[b * 128 : (b + 1) * 128, :].T for b in range(blocks)]
    rows = []
    for h in range(2):
        left = jnp.concatenate([f[h * HD : h * HD + 1, :] for f in flipped], axis=0)
        for _ in range(parts):
            piece = left.astype(BF16)
            rows.append(piece.astype(F32))
            left = left - piece.astype(F32)
    return jnp.concatenate(rows, axis=0).astype(BF16)


def pack_q_kernel(q_ref, lse_ref, out_ref):
    total = q_ref.shape[0]
    out_ref[:total, :] = q_ref[...]
    out_ref[total:, :] = column_to_rows(lse_ref[...], 3)


def pack_g_kernel(g_ref, o_ref, out_ref):
    total = g_ref.shape[0]
    g = g_ref[...]
    out_ref[:total, :] = g
    prod = g.astype(F32) * o_ref[...].astype(F32)
    sums = [jnp.sum(lanes_of(prod, h), axis=1, keepdims=True) for h in range(2)]
    out_ref[total:, :] = column_to_rows(merge(*sums), 2)


def pack_call(kernel, first, second, parts):
    total = first.shape[0]
    return pl.pallas_call(
        kernel, out_shape=jax.ShapeDtypeStruct((total + total // 128 * 2 * parts, 128), BF16)
    )(first, second)


def dq_kernel(chunks, q_ref, g_ref, o_ref, lse_ref, cos_ref, sin_ref, *refs):
    q, g = q_ref[...], g_ref[...]
    prod = g.astype(F32) * o_ref[...].astype(F32)
    lse = lse_ref[...]
    done = []
    for h in range(2):
        qh, gh = lanes_of(q, h), lanes_of(g, h)
        delta = jnp.sum(lanes_of(prod, h), axis=1, keepdims=True)
        total = jnp.zeros(q.shape, F32)
        for kv_ref in refs[:chunks]:
            k, v = kv_ref[:, :128], kv_ref[:, 128:]
            p = jnp.exp2(nt_dot(qh, k) * C2 - lse[:, h * HD : h * HD + 1])
            ds = (p * (nt_dot(gh, v) - delta)).astype(BF16)
            total = total + nn_dot(ds, k)
        done.append(total)
    dq = merge(*done) * SCALE
    refs[-1][...] = (dq * cos_ref[...] - half_turn(dq) * sin_ref[...]).astype(BF16)


def dq_call(q, g, o, lse, cos, sin, kvs, part, parts, done, rows=256):
    total, keys = q.shape[0] // parts, kvs[0].shape[0]
    steps = total // rows
    block = pl.BlockSpec((rows, 128), lambda i: (i + part * steps, 0))
    return pl.pallas_call(
        functools.partial(dq_kernel, len(kvs)),
        grid=(steps,),
        in_specs=[block] * 6
        + [pl.BlockSpec((keys, 256), lambda i: (0, 0))] * len(kvs)
        + [pl.BlockSpec(memory_space=pl.ANY)] * len(done),
        out_specs=[block],
        out_shape=[jax.ShapeDtypeStruct(q.shape, BF16)],
        input_output_aliases={6 + len(kvs) + i: i for i in range(len(done))},
        cost_estimate=pl.CostEstimate(
            flops=total * keys * len(kvs) * 256 * 6,
            transcendentals=total * keys * len(kvs) * 2,
            bytes_accessed=total * 2048 + keys * len(kvs) * 512,
        ),
        name="attend_dq",
    )(q, g, o, lse, cos, sin, *kvs, *done)


def row_of(stats, head, parts, blocks):
    base = head * parts * blocks
    pieces = [stats[base + i * blocks : base + (i + 1) * blocks, :].astype(F32) for i in range(parts)]
    whole = functools.reduce(lambda a, b: a + b, pieces)
    return jnp.concatenate([whole[b : b + 1, :] for b in range(blocks)], axis=1)


def dkv_kernel(k_ref, v_ref, cos_ref, sin_ref, q_ref, g_ref, *refs):
    dk_ref, dv_ref = refs[-2:]
    k, v = k_ref[...], v_ref[...]
    rows = k.shape[0]
    ks = [lanes_of(k, h) for h in range(2)]
    vs = [lanes_of(v, h) for h in range(2)]
    blocks = (q_ref.shape[1] - g_ref.shape[1]) // 2
    slab = blocks * 128

    def step(j, carry):
        q = q_ref[j, :slab, :]
        g = g_ref[j, :slab, :]
        lse = q_ref[j, slab:, :].astype(F32)
        delta = g_ref[j, slab:, :].astype(F32)
        new = []
        for h in range(2):
            dk, dv = carry[h]
            p = jnp.exp2(nt_dot(ks[h], q) * C2 - row_of(lse, h, 3, blocks))
            ds = (p * (nt_dot(vs[h], g) - row_of(delta, h, 2, blocks))).astype(BF16)
            dv = dv + nn_dot(p.astype(BF16), g)
            dk = dk + nn_dot(ds, q)
            new.append((dk, dv))
        return tuple(new)

    zero = jnp.zeros((rows, 128), F32)
    done = lax.fori_loop(0, q_ref.shape[0], step, ((zero, zero), (zero, zero)))
    dk = merge(done[0][0], done[1][0]) * SCALE
    dk_ref[...] = (dk * cos_ref[...] - half_turn(dk) * sin_ref[...]).astype(BF16)
    dv_ref[...] = merge(done[0][1], done[1][1]).astype(BF16)


def dkv_call(kv, cos, sin, q_all, g_all, part, parts, done, rows=256):
    total = kv.shape[0] // parts
    slab = kv.shape[0] * q_all.shape[0]
    steps = total // rows
    block = pl.BlockSpec((rows, 128), lambda i: (i + part * steps, 0))
    return pl.pallas_call(
        dkv_kernel,
        grid=(steps,),
        in_specs=[
            block,
            pl.BlockSpec((rows, 128), lambda i: (i + part * steps, 1)),
            block,
            block,
            pl.BlockSpec(q_all.shape, lambda i: (0, 0, 0)),
            pl.BlockSpec(g_all.shape, lambda i: (0, 0, 0)),
        ]
        + [pl.BlockSpec(memory_space=pl.ANY)] * len(done),
        out_specs=[block] * 2,
        out_shape=[jax.ShapeDtypeStruct((kv.shape[0], 128), BF16)] * 2,
        input_output_aliases={6 + i: i for i in range(len(done))},
        cost_estimate=pl.CostEstimate(
            flops=total * slab * 256 * 8,
            transcendentals=total * slab * 2,
            bytes_accessed=total * 2048 + slab * 512,
        ),
        name="attend_dkv",
    )(kv, kv, cos, sin, q_all, g_all, *done)


def mlp_grads_kernel(down, at_ref, *refs):
    mine_ref, other_ref, w_ref = refs[:3]
    outs = refs[-3:] if down % 128 == 0 else refs[-2:]
    data = jnp.where(pl.program_id(0) == 0, mine_ref[...], other_ref[...])
    rows = outs[0].shape[0]
    nf = (data.shape[0] - down) // (2 * rows)
    ff = outs[0].shape[1] // (2 * nf)
    for f in range(nf):
        for g in range(2):
            first = (2 * f + g) * rows
            column = (g * nf + f) * ff
            outs[0][:, column : column + ff] = data[first : first + rows, :ff].astype(F32)
    product = outs[0][...] * w_ref[...].astype(F32)
    total = jnp.sum(product, axis=1, keepdims=True)
    outs[1][...] = jnp.broadcast_to(total, outs[1].shape)
    if down % 128 == 0:
        outs[2][...] = data[2 * nf * rows :, :].astype(F32).T[:ff, :]


def mlp_grads_call(at, mine, other, w_in, done, chunks, columns, ff):
    rows = w_in.shape[0] // chunks
    whole = pl.BlockSpec(mine.shape, lambda i, at: (0, 0))
    specs = [
        pl.BlockSpec((rows, w_in.shape[1]), lambda i, at: (at[i], 0)),
        pl.BlockSpec((rows, 128), lambda i, at: (at[i], 0)),
    ]
    shapes = [
        jax.ShapeDtypeStruct(w_in.shape, F32),
        jax.ShapeDtypeStruct((w_in.shape[0], 128), F32),
    ]
    if columns % 128 == 0:
        specs.append(pl.BlockSpec((ff, columns), lambda i, at: (0, at[i])))
        shapes.append(jax.ShapeDtypeStruct((ff, columns * chunks), F32))
    return pl.pallas_call(
        functools.partial(mlp_grads_kernel, columns),
        grid_spec=pltpu.PrefetchScalarGridSpec(
            num_scalar_prefetch=1,
            grid=(2,),
            in_specs=[whole, whole, specs[0]] + [pl.BlockSpec(memory_space=pl.ANY)] * len(done),
            out_specs=specs,
        ),
        out_shape=shapes,
        input_output_aliases={4 + i: i for i in range(len(done))},
        name="mlp_grads",
    )(at, mine, other, w_in, *done)


def attn_grads_kernel(at_ref, mine_ref, other_ref, w_ref, *refs):
    dqkv_ref, gain_ref, dout_ref = refs[-3:]
    rows, lo = dqkv_ref.shape[0], dout_ref.shape[0]
    nf = dqkv_ref.shape[1] // (3 * lo * 128)
    swapped = at_ref[1] == 1
    data = [
        jnp.where(swapped, other_ref[...], mine_ref[...]),
        jnp.where(swapped, mine_ref[...], other_ref[...]),
    ]
    total = jnp.zeros((rows, 1), F32)
    for j in range(3):
        for f in range(nf):
            first = (f * 3 + j) * rows
            for l in range(lo):
                at = (j * nf * lo + f * lo + l) * 128
                piece = data[l][first : first + rows, :].astype(F32)
                dqkv_ref[:, at : at + 128] = piece
                weights = w_ref[:, at : at + 128].astype(F32)
                total = total + jnp.sum(piece * weights, axis=1, keepdims=True)
    gain_ref[...] = jnp.broadcast_to(total, gain_ref.shape)
    base, some = nf * 3 * rows, dout_ref.shape[1]
    for l in range(lo):
        for b in range(dout_ref.shape[2] // 128):
            first = base + b * some
            piece = data[l][first : first + some, :].astype(F32)
            dout_ref[l, :, b * 128 : b * 128 + 128] = piece


def attn_grads_call(at, mine, other, w_qkv, done, hi, lo, width):
    per, columns = w_qkv.shape
    rows, some = per // hi, per // hi // lo
    whole = pl.BlockSpec(mine.shape, lambda i, at: (0, 0))
    return pl.pallas_call(
        attn_grads_kernel,
        grid_spec=pltpu.PrefetchScalarGridSpec(
            num_scalar_prefetch=1,
            grid=(1,),
            in_specs=[whole, whole, pl.BlockSpec((rows, columns), lambda i, at: (at[0], 0))]
            + [pl.BlockSpec(memory_space=pl.ANY)] * len(done),
            out_specs=[
                pl.BlockSpec((rows, columns), lambda i, at: (at[0], 0)),
                pl.BlockSpec((rows, 128), lambda i, at: (at[0], 0)),
                pl.BlockSpec((lo, some, width), lambda i, at: (0, at[0], 0)),
            ],
        ),
        out_shape=[
            jax.ShapeDtypeStruct((per, columns), F32),
            jax.ShapeDtypeStruct((per, 128), F32),
            jax.ShapeDtypeStruct((lo, per // lo, width), F32),
        ],
        input_output_aliases={4 + i: i for i in range(len(done))},
        name="attn_grads",
    )(at, mine, other, w_qkv, *done)


def gelu_parts(inner):
    phi = 0.5 * (1.0 + lax.erf(inner * SQRT_HALF))
    slope = phi + inner * jnp.exp(-0.5 * inner * inner) * INV_SQRT_TAU
    return inner * phi, slope


def exchange(parts, axes):
    return lax.all_to_all(parts, axes, 0, 0, tiled=True)


def swap_lo(values):
    return lax.ppermute(values, "lo", [(0, 1), (1, 0)])


def pick(values, axis, index):
    return lax.dynamic_index_in_dim(values, index, axis, keepdims=False)


def fence(*values):
    return lax.optimization_barrier(values)


def on_device(x, gain_attn, w_qkv, w_out, gain_mlp, w_in, w_down, cotangent):
    lo, nf, hi = lax.axis_size("lo"), lax.axis_size("fsdp"), lax.axis_size("hi")
    rows, width = x.shape
    slab = rows * lo * nf
    here = lax.axis_index("lo")
    ff = w_down.shape[0]
    wide = -(-ff // 128) * 128
    w_down = jnp.pad(w_down, ((0, wide - ff), (0, 0)))

    x_slab = lax.all_gather(x, SLAB, axis=0, tiled=True)
    gains = lax.all_gather(jnp.stack([gain_attn, gain_mlp]), "fsdp", axis=1, tiled=True)
    gain_one, gain_two = gains[:1].astype(F32), gains[1:].astype(F32)
    wq = pick(w_qkv.reshape(-1, 3, nf, lo, 128), 3, here)
    wq = wq.transpose(2, 0, 1, 3).reshape(nf, -1, 384)
    wq = exchange(wq, "fsdp").reshape(width, 384)
    out_full = lax.all_gather(w_out, "fsdp", axis=0, tiled=True)
    wi = w_in.reshape(-1, 2, nf, ff).transpose(2, 1, 0, 3)

    first = lax.axis_index("hi") * slab
    half = HD // 2
    freq = THETA ** (-((jnp.arange(128) % half).astype(F32) * 2.0 / HD))
    angle = (first + jnp.arange(slab)).astype(F32)[:, None] * freq[None, :]
    cos, sin = jnp.cos(angle), jnp.sin(angle)

    wq, wi, cos, sin = fence(wq, wi, cos, sin)
    xn1_slab, q, kv = qkv_call(x_slab, gain_one, wq, cos, sin)
    ct_all = lax.all_gather(cotangent, "fsdp", axis=0, tiled=True)
    ring = [(i, (i + 1) % hi) for i in range(hi)]
    kvs, state = [kv], ()
    for i in range(hi):
        last = i == hi - 1
        if not last:
            after = lax.ppermute(kvs[i], "hi", ring)
        else:
            q, wi = fence(q, wi)
        state = attend_call(q, kvs[i], state, last)
        if i == 0:
            state, wi = fence(state, wi)
            wi = exchange(wi, "fsdp")
        if not last:
            after, state = fence(after, state)
            kvs.append(after)
    o, lse = state
    w_a, w_b = [
        jnp.pad(wi[:, g].reshape(width, ff), ((0, 0), (0, wide - ff))) for g in range(2)
    ]

    q_pack = pack_call(pack_q_kernel, q, lse, 3)
    at_hi = lax.axis_index("hi")
    q_all = jnp.zeros((hi,) + q_pack.shape, BF16)
    for step in range(hi):
        q_all = lax.dynamic_update_index_in_dim(q_all, q_pack, (at_hi - step) % hi, 0)
        if step < hi - 1:
            q_pack = lax.ppermute(q_pack, "hi", ring)

    o_pair = o.reshape(lo, nf * rows, 128)
    o_mine, o_other = pick(o_pair, 0, here), swap_lo(pick(o_pair, 0, 1 - here))
    o_four = jnp.concatenate(
        [jnp.where(here == 0, o_mine, o_other), jnp.where(here == 0, o_other, o_mine)], axis=1
    )

    o_own = exchange(o.reshape(lo * nf, rows, 128), SLAB)
    o_own = o_own.reshape(lo, nf, rows, 128).transpose(2, 1, 0, 3).reshape(rows, width)
    xf = x.astype(F32)
    hidden = xf + nn_dot(o_own, out_full)
    xn2, n2, r2 = layer_norm(hidden, gain_two)
    xn2_all = lax.all_gather(xn2.astype(BF16), "fsdp", axis=0, tiled=True)
    xn2_all, o_four = fence(xn2_all, o_four)

    a, b = nn_dot(xn2_all, w_a), nn_dot(xn2_all, w_b)
    act, slope = gelu_parts(a)
    u = (act * b).astype(BF16)
    du = nt_dot(ct_all, w_down)
    da = (du * b * slope).astype(BF16)
    db = (du * act).astype(BF16)

    per, chunks = width // nf, lo * hi

    def halves(p):
        p = p.reshape((lo, hi) + p.shape[1:])
        return pick(p, 0, here), pick(p, 0, 1 - here)

    def over_hi_scattered(total):
        return lax.psum_scatter(total, "hi", scatter_dimension=0, tiled=True)[0]

    per, chunks = width // nf, lo * hi

    def halves(p):
        p = p.reshape((lo, hi) + p.shape[1:])
        return pick(p, 0, here), pick(p, 0, 1 - here)

    def added(own, other):
        return (own.astype(F32) + other.astype(F32)).astype(BF16)

    def over_hi_scattered(total):
        return lax.psum_scatter(total, "hi", scatter_dimension=0, tiled=True)[0]

    def fold(p, axis, bit):
        mine = lax.axis_index("fsdp") // bit % 2
        other = lax.ppermute(
            pick(p, axis, 1 - mine), "fsdp", [(i, i ^ bit) for i in range(nf)]
        )
        return added(pick(p, axis, mine), other)

    d_xn2 = nt_dot(da, w_a) + nt_dot(db, w_b)
    d_xn2 = fold(d_xn2.astype(BF16).reshape(2, 2, rows, width), 1, 1)
    p_down = halves(tn_dot(ct_all, u).astype(BF16).reshape(chunks, -1, wide))
    mine = lax.axis_index("fsdp") // 2
    d_other = lax.ppermute(pick(d_xn2, 0, 1 - mine), "fsdp", [(i, i ^ 2) for i in range(nf)])
    d_xn2 = pick(d_xn2, 0, mine)
    t_down = swap_lo(p_down[1])
    p_in = jnp.stack([tn_dot(xn2_all, da), tn_dot(xn2_all, db)], axis=1).astype(BF16)
    p_in = p_in.reshape(nf, chunks, per // chunks, 2, wide).transpose(1, 0, 3, 2, 4)
    p_in = halves(p_in.reshape(chunks, -1, wide))
    d_other, p_in = fence(d_other, p_in)

    d_xn2 = d_xn2.astype(F32) + d_other.astype(F32)
    d_hidden = cotangent.astype(F32) + norm_back(d_xn2, n2, r2, gain_two)
    dhb = d_hidden.astype(BF16)
    d_o = nt_dot(dhb, out_full).astype(BF16)
    d_o = d_o.reshape(rows, nf, lo, 128).transpose(2, 1, 0, 3).reshape(lo * nf, rows, 128)
    d_o, own_down = fence(d_o, p_down[0])
    t_down = added(own_down, t_down)
    d_o, t_down = fence(d_o, t_down)

    def down_part(step):
        return pick(t_down, 0, (at_hi - 1 - step) % hi)

    def down_hop(total):
        return lax.ppermute(total, "hi", ring)

    r_down = down_hop(down_part(0))
    dhb_all = lax.all_gather(dhb, "fsdp", axis=0, tiled=True)
    grads = exchange(d_o, SLAB).reshape(slab, 128)
    p_out = halves(tn_dot(o_four, dhb_all).astype(BF16).reshape(chunks, -1, width))
    t_out = swap_lo(p_out[1])
    grads, p_in, q_all, t_down, p_out = fence(grads, p_in, q_all, t_down, p_out)
    t_in = swap_lo(p_in[1])
    g_pack = pack_call(pack_g_kernel, grads, o, 2)
    r_down, g_pack = fence(r_down, g_pack)
    g_all = lax.all_gather(g_pack, "hi", axis=0)
    if hi > 2:
        r_down = down_hop(added(down_part(1), r_down))
    dq = dq_call(q, grads, o, lse, cos, sin, kvs, 0, 1, ())[0]
    u, dq, r_down, t_out = fence(u, dq, r_down, t_out)
    for step in range(2, hi - 1):
        r_down = down_hop(added(down_part(step), r_down))
    t_out = added(p_out[0], t_out)
    out_part = nn_dot(u, w_down).astype(BF16).reshape(nf, rows, width)
    out_part = exchange(out_part, "fsdp")
    g_all, t_out = fence(g_all, t_out)
    r_out = over_hi_scattered(t_out)
    dkv = dkv_call(kv, cos, sin, q_all, g_all, 0, 2, ())
    dkv, t_in, own_in, r_down = fence(dkv, t_in, p_in[0], r_down)
    r_down = added(down_part(hi - 1), r_down)
    t_in = added(own_in, t_in)
    dkv, t_in, r_out = fence(dkv, t_in, r_out)
    r_in = over_hi_scattered(t_in)
    dk, dv = dkv_call(kv, cos, sin, q_all, g_all, 1, 2, dkv)
    dk, out_part = fence(dk, out_part)

    dqkv = jnp.concatenate([dq, dk, dv], axis=1)
    p_qkv = tn_dot(xn1_slab, dqkv).astype(BF16)
    p_qkv = p_qkv.reshape(nf, hi, per // hi, 384).transpose(1, 0, 2, 3)
    p_qkv = exchange(p_qkv.reshape(hi * nf, per // hi, 384), ("hi", "fsdp"))
    d_xn1 = nt_dot(dqkv, wq).astype(BF16).reshape(lo, 2, 2, rows, width)
    d_xn1 = fold(d_xn1, 2, 1)
    d_xn1, r_in = fence(d_xn1, r_in)

    split = r_in.shape[0]
    r_in = r_in.reshape(nf, -1, wide)
    at_f = lax.axis_index("fsdp")
    turned = r_in
    for bit in range(1, nf):
        piece = lax.ppermute(pick(r_in, 0, at_f ^ bit), "fsdp", [(i, i ^ bit) for i in range(nf)])
        turned = lax.dynamic_update_index_in_dim(turned, piece, at_f ^ bit, 0)
    turned, d_xn1 = fence(turned, d_xn1)
    mlp = jnp.concatenate([turned.reshape(split, wide), r_down], axis=0)

    done, placed, downs = (), (), jnp.zeros((chunks, width // chunks, wide), BF16)

    def hop(p):
        return lax.ppermute(p, "hi", ring)

    def mlp_place(step, mine, other):
        at = (at_hi - step) % hi
        at = jnp.stack([here * hi + at, (1 - here) * hi + at])
        return mlp_grads_call(at, mine, other, w_in, done, chunks, width // chunks, ff), at

    def attn_place(step, mine, other):
        at = jnp.stack([(at_hi - step) % hi, here])
        return attn_grads_call(at, mine, other, w_qkv, placed, hi, lo, width)

    mlp_done = attn_done = None
    attn = attn_other = ()
    for step in range(hi + 1):
        flight = {}
        if step < hi:
            flight["mlp_other"] = swap_lo(mlp)
        if step < hi - 1:
            flight["mlp"] = hop(mlp)
        turn = step - 1
        if 0 <= turn < hi:
            flight["attn_other"] = hop(attn_other) if 0 < turn >= hi - 2 else swap_lo(attn)
        if 0 <= turn < hi - 1:
            flight["attn"] = hop(attn)
        if step == 0:
            total = jnp.sum(p_qkv.reshape(hi, -1, 3, 128).astype(F32), axis=0).astype(BF16)
            r_out = r_out.reshape(-1, width // 128, 128).transpose(1, 0, 2).reshape(-1, 128)
            total = total.reshape(nf, -1, 3, 128).transpose(0, 2, 1, 3).reshape(-1, 128)
            flight["payload"] = jnp.concatenate([total, r_out], axis=0)
            d_xn1 = fold(d_xn1, 1, 2)
            flight["x"] = d_xn1
        if step == hi:
            flight["x"] = swap_lo(pick(d_xn1, 0, 1 - here))
        if mlp_done:
            done, at = mlp_place(*mlp_done)
            if len(done) == 2:
                for index, piece in zip(at, mlp_done[1:]):
                    downs = lax.dynamic_update_index_in_dim(downs, piece[split:], index, 0)
        if attn_done:
            placed = attn_place(*attn_done)
        held = {"mlp": mlp, "attn": attn, "done": done, "placed": placed}
        flight, held = fence(flight, held)
        done, placed = held["done"], held["placed"]
        mlp_done = (step, held["mlp"], flight["mlp_other"]) if step < hi else None
        attn_done = (turn, held["attn"], flight["attn_other"]) if 0 <= turn < hi else None
        mlp, attn = flight.get("mlp"), flight.get("attn", ())
        attn_other = flight.get("attn_other", ())
        if step == 0:
            attn = flight["payload"]
            d_xn1 = flight["x"]
        if step == hi:
            own_x, other_x = pick(d_xn1, 0, here), flight["x"]
    if attn_done:
        placed = attn_place(*attn_done)
    if len(done) == 3:
        d_w_down = done[2]
    else:
        d_w_down = downs.reshape(width, wide)[:, :ff].T.astype(F32)
    d_w_in = done[0]
    d_w_qkv, gain_sum, d_w_out = placed[0], placed[1][:, 0], placed[2].reshape(per, width)

    out_sum = jnp.sum(out_part.astype(F32), axis=0)
    output = (hidden + out_sum).astype(BF16)

    d_xn1 = own_x.astype(F32) + other_x.astype(F32)
    _, n1, r1 = layer_norm(xf, gain_one)
    d_x = d_hidden + norm_back(d_xn1, n1, r1, gain_one)

    d_gain_attn = gain_sum / gain_attn.astype(F32)
    d_gain_mlp = done[1][:, 0] / gain_mlp.astype(F32)
    return (output, d_x, d_gain_attn, d_gain_mlp, d_w_qkv, d_w_out, d_w_in, d_w_down)


def solution(mesh):
    ctx, fsdp = mesh.shape["ctx"], mesh.shape["fsdp"]
    lo = H // 2 // fsdp
    split = Mesh(mesh.devices.reshape(ctx // lo, lo, fsdp), ("hi", "lo", "fsdp"))
    tokens = P(("hi", "lo", "fsdp"), None)
    shards = P("fsdp", None)

    return jax.shard_map(
        on_device,
        mesh=split,
        in_specs=(tokens, P("fsdp"), shards, shards, P("fsdp"), shards, shards, tokens),
        out_specs=(tokens, tokens, P("fsdp"), P("fsdp"), shards, shards, shards, shards),
        check_vma=False,
    )
```

```python
import functools

import jax
import jax.numpy as jnp
from jax import lax
from jax.experimental import pallas as pl
from jax.experimental.pallas import tpu as pltpu
from jax.sharding import Mesh, PartitionSpec as P


H = 16
HD = 64
EPS = 1e-05
THETA = 160000.0
SQRT_HALF = 0.7071067811865476
INV_SQRT_TAU = 0.3989422804014327
LOG2E = 1.4426950408889634
SCALE = 0.125
C2 = SCALE * LOG2E
F32 = jnp.float32
BF16 = jnp.bfloat16
SLAB = ("lo", "fsdp")


def nt_dot(a, b):
    return lax.dot_general(a, b, (((1,), (1,)), ((), ())), preferred_element_type=F32)


def tn_dot(a, b):
    return lax.dot_general(a, b, (((0,), (0,)), ((), ())), preferred_element_type=F32)


def nn_dot(a, b):
    return jnp.dot(a, b, preferred_element_type=F32)


def layer_norm(values, gain):
    middle = jnp.mean(values, axis=-1, keepdims=True)
    centered = values - middle
    spread = jnp.mean(centered * centered, axis=-1, keepdims=True)
    inverse = lax.rsqrt(spread + EPS)
    normed = centered * inverse
    return (normed * gain, normed, inverse)


def norm_back(incoming, normed, inverse, gain):
    scaled = incoming * gain
    return inverse * (
        scaled
        - jnp.mean(scaled, axis=-1, keepdims=True)
        - normed * jnp.mean(scaled * normed, axis=-1, keepdims=True)
    )


def half_turn(u):
    lane = lax.broadcasted_iota(jnp.int32, u.shape, 1)
    return jnp.where(lane % HD < HD // 2, -pltpu.roll(u, 96, 1), pltpu.roll(u, 32, 1))


def lanes_of(values, head):
    lane = lax.broadcasted_iota(jnp.int32, values.shape, 1)
    return jnp.where((lane >= HD) == (head == 1), values, jnp.zeros_like(values))


def merge(first, second):
    shape = first.shape if first.shape[1] > 1 else (first.shape[0], 128)
    lane = lax.broadcasted_iota(jnp.int32, shape, 1)
    return jnp.where(lane < HD, first, second)


def qkv_kernel(x_ref, g_ref, w_ref, cos_ref, sin_ref, xn_ref, q_ref, kv_ref):
    xn, _, _ = layer_norm(x_ref[...].astype(F32), g_ref[...])
    xnb = xn.astype(BF16)
    xn_ref[...] = xnb
    out = nn_dot(xnb, w_ref[...])
    cos, sin = cos_ref[...], sin_ref[...]
    q, k = out[:, :128], out[:, 128:256]
    q_ref[...] = (q * cos + half_turn(q) * sin).astype(BF16)
    kv_ref[:, :128] = (k * cos + half_turn(k) * sin).astype(BF16)
    kv_ref[:, 128:] = out[:, 256:].astype(BF16)


def qkv_call(x, gain, w, cos, sin, rows=256):
    total, width = x.shape
    return pl.pallas_call(
        qkv_kernel,
        grid=(total // rows,),
        in_specs=[
            pl.BlockSpec((rows, width), lambda i: (i, 0)),
            pl.BlockSpec((1, width), lambda i: (0, 0)),
            pl.BlockSpec(w.shape, lambda i: (0, 0)),
            pl.BlockSpec((rows, 128), lambda i: (i, 0)),
            pl.BlockSpec((rows, 128), lambda i: (i, 0)),
        ],
        out_specs=[
            pl.BlockSpec((rows, width), lambda i: (i, 0)),
            pl.BlockSpec((rows, 128), lambda i: (i, 0)),
            pl.BlockSpec((rows, 256), lambda i: (i, 0)),
        ],
        out_shape=[
            jax.ShapeDtypeStruct((total, width), BF16),
            jax.ShapeDtypeStruct((total, 128), BF16),
            jax.ShapeDtypeStruct((total, 256), BF16),
        ],
        name="qkv_rope",
    )(x, gain, w, cos, sin)


def attend_kernel(begin, end, q_ref, k_ref, v_ref, *refs):
    q, k, v = q_ref[...], k_ref[...], v_ref[...]
    if not begin:
        tops, masses, acc = [r[...] for r in refs[:3]]
    new = []
    for h in range(2):
        s = nt_dot(lanes_of(q, h), k)
        top = jnp.max(s, axis=1, keepdims=True)
        if not begin:
            old = tops[:, h * HD : h * HD + 1]
            top = jnp.maximum(old, top)
            keep = jnp.exp2((old - top) * C2)
        p = jnp.exp2((s - top) * C2)
        mass = jnp.sum(p, axis=1, keepdims=True)
        part = nn_dot(p.astype(BF16), v)
        if not begin:
            mass = mass + masses[:, h * HD : h * HD + 1] * keep
            part = part + acc * keep
        new.append((top, mass, part))
    if end:
        refs[-2][...] = merge(*[part / mass for _, mass, part in new]).astype(BF16)
        refs[-1][...] = merge(*[top * C2 + jnp.log2(mass) for top, mass, _ in new])
    else:
        for ref, both in zip(refs[-3:], zip(*new)):
            ref[...] = merge(*both)


def attend_call(q, kv, state, end, rows=256):
    total, keys = q.shape[0], kv.shape[0]
    block = pl.BlockSpec((rows, 128), lambda i: (i, 0))
    shapes = [BF16, F32] if end else [F32] * 3
    work = total * keys * 256 * 4
    return pl.pallas_call(
        functools.partial(attend_kernel, not state, end),
        grid=(total // rows,),
        in_specs=[
            block,
            pl.BlockSpec((keys, 128), lambda i: (0, 0)),
            pl.BlockSpec((keys, 128), lambda i: (0, 1)),
        ]
        + [block] * len(state),
        out_specs=[block] * len(shapes),
        out_shape=[jax.ShapeDtypeStruct((total, 128), t) for t in shapes],
        cost_estimate=pl.CostEstimate(
            flops=work, transcendentals=total * keys * 2, bytes_accessed=total * 4096
        ),
        name="attend",
    )(q, kv, kv, *state)


def column_to_rows(values, parts):
    blocks = values.shape[0] // 128
    flipped = [values[b * 128 : (b + 1) * 128, :].T for b in range(blocks)]
    rows = []
    for h in range(2):
        left = jnp.concatenate([f[h * HD : h * HD + 1, :] for f in flipped], axis=0)
        for _ in range(parts):
            piece = left.astype(BF16)
            rows.append(piece.astype(F32))
            left = left - piece.astype(F32)
    return jnp.concatenate(rows, axis=0).astype(BF16)


def pack_q_kernel(q_ref, lse_ref, out_ref):
    total = q_ref.shape[0]
    out_ref[:total, :] = q_ref[...]
    out_ref[total:, :] = column_to_rows(lse_ref[...], 3)


def pack_g_kernel(g_ref, o_ref, out_ref):
    total = g_ref.shape[0]
    g = g_ref[...]
    out_ref[:total, :] = g
    prod = g.astype(F32) * o_ref[...].astype(F32)
    sums = [jnp.sum(lanes_of(prod, h), axis=1, keepdims=True) for h in range(2)]
    out_ref[total:, :] = column_to_rows(merge(*sums), 2)


def pack_call(kernel, first, second, parts):
    total = first.shape[0]
    return pl.pallas_call(
        kernel, out_shape=jax.ShapeDtypeStruct((total + total // 128 * 2 * parts, 128), BF16)
    )(first, second)


def dq_kernel(chunks, q_ref, g_ref, o_ref, lse_ref, cos_ref, sin_ref, *refs):
    q, g = q_ref[...], g_ref[...]
    prod = g.astype(F32) * o_ref[...].astype(F32)
    lse = lse_ref[...]
    done = []
    for h in range(2):
        qh, gh = lanes_of(q, h), lanes_of(g, h)
        delta = jnp.sum(lanes_of(prod, h), axis=1, keepdims=True)
        total = jnp.zeros(q.shape, F32)
        for kv_ref in refs[:chunks]:
            k, v = kv_ref[:, :128], kv_ref[:, 128:]
            p = jnp.exp2(nt_dot(qh, k) * C2 - lse[:, h * HD : h * HD + 1])
            ds = (p * (nt_dot(gh, v) - delta)).astype(BF16)
            total = total + nn_dot(ds, k)
        done.append(total)
    dq = merge(*done) * SCALE
    refs[-1][...] = (dq * cos_ref[...] - half_turn(dq) * sin_ref[...]).astype(BF16)


def dq_call(q, g, o, lse, cos, sin, kvs, part, parts, done, rows=256):
    total, keys = q.shape[0] // parts, kvs[0].shape[0]
    steps = total // rows
    block = pl.BlockSpec((rows, 128), lambda i: (i + part * steps, 0))
    return pl.pallas_call(
        functools.partial(dq_kernel, len(kvs)),
        grid=(steps,),
        in_specs=[block] * 6
        + [pl.BlockSpec((keys, 256), lambda i: (0, 0))] * len(kvs)
        + [pl.BlockSpec(memory_space=pl.ANY)] * len(done),
        out_specs=[block],
        out_shape=[jax.ShapeDtypeStruct(q.shape, BF16)],
        input_output_aliases={6 + len(kvs) + i: i for i in range(len(done))},
        cost_estimate=pl.CostEstimate(
            flops=total * keys * len(kvs) * 256 * 6,
            transcendentals=total * keys * len(kvs) * 2,
            bytes_accessed=total * 2048 + keys * len(kvs) * 512,
        ),
        name="attend_dq",
    )(q, g, o, lse, cos, sin, *kvs, *done)


def row_of(stats, head, parts, blocks):
    base = head * parts * blocks
    pieces = [stats[base + i * blocks : base + (i + 1) * blocks, :].astype(F32) for i in range(parts)]
    whole = functools.reduce(lambda a, b: a + b, pieces)
    return jnp.concatenate([whole[b : b + 1, :] for b in range(blocks)], axis=1)


def dkv_kernel(k_ref, v_ref, cos_ref, sin_ref, q_ref, g_ref, *refs):
    dk_ref, dv_ref = refs[-2:]
    k, v = k_ref[...], v_ref[...]
    rows = k.shape[0]
    ks = [lanes_of(k, h) for h in range(2)]
    vs = [lanes_of(v, h) for h in range(2)]
    blocks = (q_ref.shape[1] - g_ref.shape[1]) // 2
    slab = blocks * 128

    def step(j, carry):
        q = q_ref[j, :slab, :]
        g = g_ref[j, :slab, :]
        lse = q_ref[j, slab:, :].astype(F32)
        delta = g_ref[j, slab:, :].astype(F32)
        new = []
        for h in range(2):
            dk, dv = carry[h]
            p = jnp.exp2(nt_dot(ks[h], q) * C2 - row_of(lse, h, 3, blocks))
            ds = (p * (nt_dot(vs[h], g) - row_of(delta, h, 2, blocks))).astype(BF16)
            dv = dv + nn_dot(p.astype(BF16), g)
            dk = dk + nn_dot(ds, q)
            new.append((dk, dv))
        return tuple(new)

    zero = jnp.zeros((rows, 128), F32)
    done = lax.fori_loop(0, q_ref.shape[0], step, ((zero, zero), (zero, zero)))
    dk = merge(done[0][0], done[1][0]) * SCALE
    dk_ref[...] = (dk * cos_ref[...] - half_turn(dk) * sin_ref[...]).astype(BF16)
    dv_ref[...] = merge(done[0][1], done[1][1]).astype(BF16)


def dkv_call(kv, cos, sin, q_all, g_all, part, parts, done, rows=256):
    total = kv.shape[0] // parts
    slab = kv.shape[0] * q_all.shape[0]
    steps = total // rows
    block = pl.BlockSpec((rows, 128), lambda i: (i + part * steps, 0))
    return pl.pallas_call(
        dkv_kernel,
        grid=(steps,),
        in_specs=[
            block,
            pl.BlockSpec((rows, 128), lambda i: (i + part * steps, 1)),
            block,
            block,
            pl.BlockSpec(q_all.shape, lambda i: (0, 0, 0)),
            pl.BlockSpec(g_all.shape, lambda i: (0, 0, 0)),
        ]
        + [pl.BlockSpec(memory_space=pl.ANY)] * len(done),
        out_specs=[block] * 2,
        out_shape=[jax.ShapeDtypeStruct((kv.shape[0], 128), BF16)] * 2,
        input_output_aliases={6 + i: i for i in range(len(done))},
        cost_estimate=pl.CostEstimate(
            flops=total * slab * 256 * 8,
            transcendentals=total * slab * 2,
            bytes_accessed=total * 2048 + slab * 512,
        ),
        name="attend_dkv",
    )(kv, kv, cos, sin, q_all, g_all, *done)


def mlp_grads_kernel(down, at_ref, *refs):
    mine_ref, other_ref, w_ref = refs[:3]
    outs = refs[-3:] if down % 128 == 0 else refs[-2:]
    data = jnp.where(pl.program_id(0) == 0, mine_ref[...], other_ref[...])
    rows = outs[0].shape[0]
    nf = (data.shape[0] - down) // (2 * rows)
    ff = outs[0].shape[1] // (2 * nf)
    for f in range(nf):
        for g in range(2):
            first = (2 * f + g) * rows
            column = (g * nf + f) * ff
            outs[0][:, column : column + ff] = data[first : first + rows, :ff].astype(F32)
    product = outs[0][...] * w_ref[...].astype(F32)
    total = jnp.sum(product, axis=1, keepdims=True)
    outs[1][...] = jnp.broadcast_to(total, outs[1].shape)
    if down % 128 == 0:
        outs[2][...] = data[2 * nf * rows :, :].astype(F32).T[:ff, :]


def mlp_grads_call(at, mine, other, w_in, done, chunks, columns, ff):
    rows = w_in.shape[0] // chunks
    whole = pl.BlockSpec(mine.shape, lambda i, at: (0, 0))
    specs = [
        pl.BlockSpec((rows, w_in.shape[1]), lambda i, at: (at[i], 0)),
        pl.BlockSpec((rows, 128), lambda i, at: (at[i], 0)),
    ]
    shapes = [
        jax.ShapeDtypeStruct(w_in.shape, F32),
        jax.ShapeDtypeStruct((w_in.shape[0], 128), F32),
    ]
    if columns % 128 == 0:
        specs.append(pl.BlockSpec((ff, columns), lambda i, at: (0, at[i])))
        shapes.append(jax.ShapeDtypeStruct((ff, columns * chunks), F32))
    return pl.pallas_call(
        functools.partial(mlp_grads_kernel, columns),
        grid_spec=pltpu.PrefetchScalarGridSpec(
            num_scalar_prefetch=1,
            grid=(2,),
            in_specs=[whole, whole, specs[0]] + [pl.BlockSpec(memory_space=pl.ANY)] * len(done),
            out_specs=specs,
        ),
        out_shape=shapes,
        input_output_aliases={4 + i: i for i in range(len(done))},
        name="mlp_grads",
    )(at, mine, other, w_in, *done)


def attn_grads_kernel(at_ref, mine_ref, other_ref, w_ref, *refs):
    dqkv_ref, gain_ref, dout_ref = refs[-3:]
    rows, lo = dqkv_ref.shape[0], dout_ref.shape[0]
    nf = dqkv_ref.shape[1] // (3 * lo * 128)
    swapped = at_ref[1] == 1
    data = [
        jnp.where(swapped, other_ref[...], mine_ref[...]),
        jnp.where(swapped, mine_ref[...], other_ref[...]),
    ]
    total = jnp.zeros((rows, 1), F32)
    for j in range(3):
        for f in range(nf):
            first = (f * 3 + j) * rows
            for l in range(lo):
                at = (j * nf * lo + f * lo + l) * 128
                piece = data[l][first : first + rows, :].astype(F32)
                dqkv_ref[:, at : at + 128] = piece
                weights = w_ref[:, at : at + 128].astype(F32)
                total = total + jnp.sum(piece * weights, axis=1, keepdims=True)
    gain_ref[...] = jnp.broadcast_to(total, gain_ref.shape)
    base, some = nf * 3 * rows, dout_ref.shape[1]
    for l in range(lo):
        for b in range(dout_ref.shape[2] // 128):
            first = base + b * some
            piece = data[l][first : first + some, :].astype(F32)
            dout_ref[l, :, b * 128 : b * 128 + 128] = piece


def attn_grads_call(at, mine, other, w_qkv, done, hi, lo, width):
    per, columns = w_qkv.shape
    rows, some = per // hi, per // hi // lo
    whole = pl.BlockSpec(mine.shape, lambda i, at: (0, 0))
    return pl.pallas_call(
        attn_grads_kernel,
        grid_spec=pltpu.PrefetchScalarGridSpec(
            num_scalar_prefetch=1,
            grid=(1,),
            in_specs=[whole, whole, pl.BlockSpec((rows, columns), lambda i, at: (at[0], 0))]
            + [pl.BlockSpec(memory_space=pl.ANY)] * len(done),
            out_specs=[
                pl.BlockSpec((rows, columns), lambda i, at: (at[0], 0)),
                pl.BlockSpec((rows, 128), lambda i, at: (at[0], 0)),
                pl.BlockSpec((lo, some, width), lambda i, at: (0, at[0], 0)),
            ],
        ),
        out_shape=[
            jax.ShapeDtypeStruct((per, columns), F32),
            jax.ShapeDtypeStruct((per, 128), F32),
            jax.ShapeDtypeStruct((lo, per // lo, width), F32),
        ],
        input_output_aliases={4 + i: i for i in range(len(done))},
        name="attn_grads",
    )(at, mine, other, w_qkv, *done)


def gelu_parts(inner):
    phi = 0.5 * (1.0 + lax.erf(inner * SQRT_HALF))
    slope = phi + inner * jnp.exp(-0.5 * inner * inner) * INV_SQRT_TAU
    return inner * phi, slope


def exchange(parts, axes):
    return lax.all_to_all(parts, axes, 0, 0, tiled=True)


def swap_lo(values):
    return lax.ppermute(values, "lo", [(0, 1), (1, 0)])


def pick(values, axis, index):
    return lax.dynamic_index_in_dim(values, index, axis, keepdims=False)


def fence(*values):
    return lax.optimization_barrier(values)


def on_device(x, gain_attn, w_qkv, w_out, gain_mlp, w_in, w_down, cotangent):
    lo, nf, hi = lax.axis_size("lo"), lax.axis_size("fsdp"), lax.axis_size("hi")
    rows, width = x.shape
    slab = rows * lo * nf
    here = lax.axis_index("lo")
    ff = w_down.shape[0]
    wide = -(-ff // 128) * 128
    w_down = jnp.pad(w_down, ((0, wide - ff), (0, 0)))

    x_slab = lax.all_gather(x, SLAB, axis=0, tiled=True)
    gains = lax.all_gather(jnp.stack([gain_attn, gain_mlp]), "fsdp", axis=1, tiled=True)
    gain_one, gain_two = gains[:1].astype(F32), gains[1:].astype(F32)
    wq = pick(w_qkv.reshape(-1, 3, nf, lo, 128), 3, here)
    wq = wq.transpose(2, 0, 1, 3).reshape(nf, -1, 384)
    wq = exchange(wq, "fsdp").reshape(width, 384)
    out_full = lax.all_gather(w_out, "fsdp", axis=0, tiled=True)
    wi = w_in.reshape(-1, 2, nf, ff).transpose(2, 1, 0, 3)

    first = lax.axis_index("hi") * slab
    half = HD // 2
    freq = THETA ** (-((jnp.arange(128) % half).astype(F32) * 2.0 / HD))
    angle = (first + jnp.arange(slab)).astype(F32)[:, None] * freq[None, :]
    cos, sin = jnp.cos(angle), jnp.sin(angle)

    wq, wi, cos, sin = fence(wq, wi, cos, sin)
    xn1_slab, q, kv = qkv_call(x_slab, gain_one, wq, cos, sin)
    ct_all = lax.all_gather(cotangent, "fsdp", axis=0, tiled=True)
    ring = [(i, (i + 1) % hi) for i in range(hi)]
    kvs, state = [kv], ()
    for i in range(hi):
        last = i == hi - 1
        if not last:
            after = lax.ppermute(kvs[i], "hi", ring)
        else:
            q, wi = fence(q, wi)
        state = attend_call(q, kvs[i], state, last)
        if i == 0:
            state, wi = fence(state, wi)
            wi = exchange(wi, "fsdp")
        if not last:
            after, state = fence(after, state)
            kvs.append(after)
    o, lse = state
    w_a, w_b = [
        jnp.pad(wi[:, g].reshape(width, ff), ((0, 0), (0, wide - ff))) for g in range(2)
    ]

    q_pack = pack_call(pack_q_kernel, q, lse, 3)
    at_hi = lax.axis_index("hi")
    q_all = jnp.zeros((hi,) + q_pack.shape, BF16)
    for step in range(hi):
        q_all = lax.dynamic_update_index_in_dim(q_all, q_pack, (at_hi - step) % hi, 0)
        if step < hi - 1:
            q_pack = lax.ppermute(q_pack, "hi", ring)

    o_pair = o.reshape(lo, nf * rows, 128)
    o_mine, o_other = pick(o_pair, 0, here), swap_lo(pick(o_pair, 0, 1 - here))
    o_four = jnp.concatenate(
        [jnp.where(here == 0, o_mine, o_other), jnp.where(here == 0, o_other, o_mine)], axis=1
    )

    o_own = exchange(o.reshape(lo * nf, rows, 128), SLAB)
    o_own = o_own.reshape(lo, nf, rows, 128).transpose(2, 1, 0, 3).reshape(rows, width)
    xf = x.astype(F32)
    hidden = xf + nn_dot(o_own, out_full)
    xn2, n2, r2 = layer_norm(hidden, gain_two)
    xn2_all = lax.all_gather(xn2.astype(BF16), "fsdp", axis=0, tiled=True)
    xn2_all, o_four = fence(xn2_all, o_four)

    a, b = nn_dot(xn2_all, w_a), nn_dot(xn2_all, w_b)
    act, slope = gelu_parts(a)
    u = (act * b).astype(BF16)
    du = nt_dot(ct_all, w_down)
    da = (du * b * slope).astype(BF16)
    db = (du * act).astype(BF16)

    per, chunks = width // nf, lo * hi

    def halves(p):
        p = p.reshape((lo, hi) + p.shape[1:])
        return pick(p, 0, here), pick(p, 0, 1 - here)

    def over_hi_scattered(total):
        return lax.psum_scatter(total, "hi", scatter_dimension=0, tiled=True)[0]

    per, chunks = width // nf, lo * hi

    def halves(p):
        p = p.reshape((lo, hi) + p.shape[1:])
        return pick(p, 0, here), pick(p, 0, 1 - here)

    def added(own, other):
        return (own.astype(F32) + other.astype(F32)).astype(BF16)

    def over_hi_scattered(total):
        return lax.psum_scatter(total, "hi", scatter_dimension=0, tiled=True)[0]

    def fold(p, axis, bit):
        mine = lax.axis_index("fsdp") // bit % 2
        other = lax.ppermute(
            pick(p, axis, 1 - mine), "fsdp", [(i, i ^ bit) for i in range(nf)]
        )
        return added(pick(p, axis, mine), other)

    d_xn2 = nt_dot(da, w_a) + nt_dot(db, w_b)
    d_xn2 = fold(d_xn2.astype(BF16).reshape(2, 2, rows, width), 1, 1)
    p_down = halves(tn_dot(ct_all, u).astype(BF16).reshape(chunks, -1, wide))
    mine = lax.axis_index("fsdp") // 2
    d_other = lax.ppermute(pick(d_xn2, 0, 1 - mine), "fsdp", [(i, i ^ 2) for i in range(nf)])
    d_xn2 = pick(d_xn2, 0, mine)
    t_down = swap_lo(p_down[1])
    p_in = jnp.stack([tn_dot(xn2_all, da), tn_dot(xn2_all, db)], axis=1).astype(BF16)
    p_in = p_in.reshape(nf, chunks, per // chunks, 2, wide).transpose(1, 0, 3, 2, 4)
    p_in = halves(p_in.reshape(chunks, -1, wide))
    d_other, p_in = fence(d_other, p_in)

    d_xn2 = d_xn2.astype(F32) + d_other.astype(F32)
    d_hidden = cotangent.astype(F32) + norm_back(d_xn2, n2, r2, gain_two)
    dhb = d_hidden.astype(BF16)
    d_o = nt_dot(dhb, out_full).astype(BF16)
    d_o = d_o.reshape(rows, nf, lo, 128).transpose(2, 1, 0, 3).reshape(lo * nf, rows, 128)
    d_o, own_down = fence(d_o, p_down[0])
    t_down = added(own_down, t_down)
    d_o, t_down = fence(d_o, t_down)

    def down_part(step):
        return pick(t_down, 0, (at_hi - 1 - step) % hi)

    def down_hop(total):
        return lax.ppermute(total, "hi", ring)

    r_down = down_hop(down_part(0))
    dhb_all = lax.all_gather(dhb, "fsdp", axis=0, tiled=True)
    grads = exchange(d_o, SLAB).reshape(slab, 128)
    p_out = halves(tn_dot(o_four, dhb_all).astype(BF16).reshape(chunks, -1, width))
    t_out = swap_lo(p_out[1])
    grads, p_in, q_all, t_down, p_out = fence(grads, p_in, q_all, t_down, p_out)
    t_in = swap_lo(p_in[1])
    g_pack = pack_call(pack_g_kernel, grads, o, 2)
    r_down, g_pack = fence(r_down, g_pack)
    g_all = lax.all_gather(g_pack, "hi", axis=0)
    if hi > 2:
        r_down = down_hop(added(down_part(1), r_down))
    dq = dq_call(q, grads, o, lse, cos, sin, kvs, 0, 1, ())[0]
    u, dq, r_down, t_out = fence(u, dq, r_down, t_out)
    for step in range(2, hi - 1):
        r_down = down_hop(added(down_part(step), r_down))
    t_out = added(p_out[0], t_out)
    out_part = nn_dot(u, w_down).astype(BF16).reshape(nf, rows, width)
    out_part = exchange(out_part, "fsdp")
    dkv = dkv_call(kv, cos, sin, q_all, g_all, 0, 2, ())
    dkv, t_in, own_in, r_down = fence(dkv, t_in, p_in[0], r_down)
    r_down = added(down_part(hi - 1), r_down)
    t_in = added(own_in, t_in)
    dkv, t_in = fence(dkv, t_in)
    r_in = over_hi_scattered(t_in)
    dk, dv = dkv_call(kv, cos, sin, q_all, g_all, 1, 2, dkv)
    dk, out_part, t_out = fence(dk, out_part, t_out)
    r_out = over_hi_scattered(t_out)

    dqkv = jnp.concatenate([dq, dk, dv], axis=1)
    p_qkv = tn_dot(xn1_slab, dqkv).astype(BF16)
    p_qkv = p_qkv.reshape(nf, hi, per // hi, 384).transpose(1, 0, 2, 3)
    p_qkv = exchange(p_qkv.reshape(hi * nf, per // hi, 384), ("hi", "fsdp"))
    d_xn1 = nt_dot(dqkv, wq).astype(BF16).reshape(lo, 2, 2, rows, width)
    d_xn1 = fold(d_xn1, 2, 1)
    d_xn1, r_in = fence(d_xn1, r_in)

    split = r_in.shape[0]
    r_in = r_in.reshape(nf, -1, wide)
    at_f = lax.axis_index("fsdp")
    turned = r_in
    for bit in range(1, nf):
        piece = lax.ppermute(pick(r_in, 0, at_f ^ bit), "fsdp", [(i, i ^ bit) for i in range(nf)])
        turned = lax.dynamic_update_index_in_dim(turned, piece, at_f ^ bit, 0)
    turned, d_xn1 = fence(turned, d_xn1)
    mlp = jnp.concatenate([turned.reshape(split, wide), r_down], axis=0)

    done, placed, downs = (), (), jnp.zeros((chunks, width // chunks, wide), BF16)

    def hop(p):
        return lax.ppermute(p, "hi", ring)

    def mlp_place(step, mine, other):
        at = (at_hi - step) % hi
        at = jnp.stack([here * hi + at, (1 - here) * hi + at])
        return mlp_grads_call(at, mine, other, w_in, done, chunks, width // chunks, ff), at

    def attn_place(step, mine, other):
        at = jnp.stack([(at_hi - step) % hi, here])
        return attn_grads_call(at, mine, other, w_qkv, placed, hi, lo, width)

    mlp_done = attn_done = None
    attn = attn_other = ()
    for step in range(hi + 1):
        flight = {}
        if step < hi:
            flight["mlp_other"] = swap_lo(mlp)
        if step < hi - 1:
            flight["mlp"] = hop(mlp)
        turn = step - 1
        if 0 <= turn < hi:
            flight["attn_other"] = hop(attn_other) if 0 < turn >= hi - 2 else swap_lo(attn)
        if 0 <= turn < hi - 1:
            flight["attn"] = hop(attn)
        if step == 0:
            total = jnp.sum(p_qkv.reshape(hi, -1, 3, 128).astype(F32), axis=0).astype(BF16)
            r_out = r_out.reshape(-1, width // 128, 128).transpose(1, 0, 2).reshape(-1, 128)
            total = total.reshape(nf, -1, 3, 128).transpose(0, 2, 1, 3).reshape(-1, 128)
            flight["payload"] = jnp.concatenate([total, r_out], axis=0)
            d_xn1 = fold(d_xn1, 1, 2)
            flight["x"] = d_xn1
        if step == hi:
            flight["x"] = swap_lo(pick(d_xn1, 0, 1 - here))
        if mlp_done:
            done, at = mlp_place(*mlp_done)
            if len(done) == 2:
                for index, piece in zip(at, mlp_done[1:]):
                    downs = lax.dynamic_update_index_in_dim(downs, piece[split:], index, 0)
        if attn_done:
            placed = attn_place(*attn_done)
        held = {"mlp": mlp, "attn": attn, "done": done, "placed": placed}
        flight, held = fence(flight, held)
        done, placed = held["done"], held["placed"]
        mlp_done = (step, held["mlp"], flight["mlp_other"]) if step < hi else None
        attn_done = (turn, held["attn"], flight["attn_other"]) if 0 <= turn < hi else None
        mlp, attn = flight.get("mlp"), flight.get("attn", ())
        attn_other = flight.get("attn_other", ())
        if step == 0:
            attn = flight["payload"]
            d_xn1 = flight["x"]
        if step == hi:
            own_x, other_x = pick(d_xn1, 0, here), flight["x"]
    if attn_done:
        placed = attn_place(*attn_done)
    if len(done) == 3:
        d_w_down = done[2]
    else:
        d_w_down = downs.reshape(width, wide)[:, :ff].T.astype(F32)
    d_w_in = done[0]
    d_w_qkv, gain_sum, d_w_out = placed[0], placed[1][:, 0], placed[2].reshape(per, width)

    out_sum = jnp.sum(out_part.astype(F32), axis=0)
    output = (hidden + out_sum).astype(BF16)

    d_xn1 = own_x.astype(F32) + other_x.astype(F32)
    _, n1, r1 = layer_norm(xf, gain_one)
    d_x = d_hidden + norm_back(d_xn1, n1, r1, gain_one)

    d_gain_attn = gain_sum / gain_attn.astype(F32)
    d_gain_mlp = done[1][:, 0] / gain_mlp.astype(F32)
    return (output, d_x, d_gain_attn, d_gain_mlp, d_w_qkv, d_w_out, d_w_in, d_w_down)


def solution(mesh):
    ctx, fsdp = mesh.shape["ctx"], mesh.shape["fsdp"]
    lo = H // 2 // fsdp
    split = Mesh(mesh.devices.reshape(ctx // lo, lo, fsdp), ("hi", "lo", "fsdp"))
    tokens = P(("hi", "lo", "fsdp"), None)
    shards = P("fsdp", None)

    return jax.shard_map(
        on_device,
        mesh=split,
        in_specs=(tokens, P("fsdp"), shards, shards, P("fsdp"), shards, shards, tokens),
        out_specs=(tokens, tokens, P("fsdp"), P("fsdp"), shards, shards, shards, shards),
        check_vma=False,
    )
```
